256 devices in a mesh: dp: 16 (over y_hi, x, core), seq: 16 (over y_lo, z).
Axes of the slice: x: 4, y: 4 (y_hi: 2, y_lo: 2; y = y_hi * 2 + y_lo), z: 8, core: 2. Of those that a mesh axis runs over, the one named last changes fastest.
Arguments:
- queries: bfloat16 [32768, 1280], P(('dp', 'seq')), may hold values from -6 to 6
- key_states: bfloat16 [32768, 1280], P(('dp', 'seq')), may hold values from -6 to 6
- value_states: bfloat16 [32768, 1280], P(('dp', 'seq')), may hold values from -6 to 6
- out_grads: bfloat16 [32768, 1280], P(('dp', 'seq')), may hold values from -6 to 6
- row_order: int32 [32768], P(('dp', 'seq')), may hold values from 0 to 127, as said below
- segment_ids: int32 [16, 2048], P('dp'), may hold values from 0 to 1, as said below
Outputs:
- grad_queries: bfloat16 [32768, 1280], P(('dp', 'seq'))
- grad_keys: bfloat16 [32768, 1280], P(('dp', 'seq'))
- grad_values: bfloat16 [32768, 1280], P(('dp', 'seq'))
The draws below stay inside these ranges and needn't reach their ends.
Inputs may be any that keep to these rules, and one draw needn't show every extreme that they name: `row_order`: each block of 128 entries names every number of 0 to 127 once. `segment_ids`: each row holds two screenshots: ids 0 then 1, never falling; the first row with id 1 lies between 768 and 1280.
All inputs are finite; a program needn't handle non-finite values.
Results may differ from the reference program's by a relative error of at most 0.012.
Values may be sent and summed in bfloat16 or wider, within the bound.
A program may use at most 64 MiB of HBM per device.

```python
import math
import jax
import jax.numpy as jnp
from jax import lax

H = 16
HD = 80
D = 1280
TOK_DEV = 128
GROUPS = 16
GROUP_ROWS = 2048
SLICE = 8
TOKENS = 32768
N_DP = 16
N_SEQ = 16


def order_table(key):
    device_keys = jax.random.split(jax.random.fold_in(key, 101), TOKENS // TOK_DEV)
    return jax.vmap(lambda device_key: jax.random.permutation(device_key, TOK_DEV))(device_keys).astype(jnp.int32)


def segment_table(key):
    cuts = jax.random.randint(jax.random.fold_in(key, 202), (GROUPS, 1), 3 * GROUP_ROWS // 8, 5 * GROUP_ROWS // 8 + 1)
    positions = jnp.arange(GROUP_ROWS)
    return (positions[None, :] >= cuts).astype(jnp.int32)


def paired_states(key):
    base = jax.random.fold_in(key, 303)
    query_part = jnp.clip(jax.random.normal(jax.random.fold_in(base, 6), (TOKENS, D)), -6.0, 6.0)
    key_part = jnp.clip(jax.random.normal(jax.random.fold_in(base, 7), (TOKENS, D)), -6.0, 6.0)
    return (query_part, key_part)


def draw_queries(key, part):
    return paired_states(key)[0].astype(jnp.bfloat16)


def draw_key_states(key, part):
    return paired_states(key)[1].astype(jnp.bfloat16)


def draw_row_order(key, part):
    return order_table(key).reshape(-1)


def draw_segment_ids(key, part):
    return segment_table(key)


def level_of(key, extent, shards, low, top_value):
    loudness = 1.0
    for position, blocks in shards:
        heights = jax.random.uniform(jax.random.fold_in(jax.random.fold_in(key, 6), position), (blocks,), jnp.float32, low / len(shards), top_value / len(shards))
        loudness = loudness * jnp.repeat(jnp.exp(heights), extent[position] // blocks).reshape((-1,) + (1,) * (len(extent) - 1 - position))
    return loudness


def scatter_about(own_key, dims, deviation, reach, cuts=(), kind=jnp.bfloat16):
    gain = level_of(own_key, dims, cuts, -0.22, 0.18) if cuts else 1.0
    values = jax.random.normal(own_key, dims, jnp.float32) * deviation * gain
    return jnp.minimum(jnp.maximum(values, -reach), reach).astype(kind)


def setup_inputs(seed: int = 0) -> dict:
    key_list = jax.random.split(jax.random.key(seed), 7)
    return {
        "queries": draw_queries(jax.random.fold_in(key_list[6], 71), 0),
        "key_states": draw_key_states(jax.random.fold_in(key_list[6], 71), 0),
        "value_states": scatter_about(key_list[2], (TOKENS, D), 1.0, 6.0, ((0, 256),)),
        "out_grads": scatter_about(key_list[3], (TOKENS, D), 1.0, 6.0, ((0, 256),)),
        "row_order": draw_row_order(jax.random.fold_in(key_list[6], 71), 0),
        "segment_ids": draw_segment_ids(jax.random.fold_in(key_list[6], 71), 0),
    }


def head_grads(head_q, head_k, head_v, head_g, matched, inv_root):
    scores = jnp.dot(head_q, head_k.T, preferred_element_type=jnp.float32) * inv_root
    scores = jnp.where(matched, scores, -1e+30)
    shifted = jnp.exp(scores - lax.optimization_barrier(jnp.max(scores, axis=-1, keepdims=True)))
    probs = shifted / lax.optimization_barrier(jnp.sum(shifted, axis=-1, keepdims=True))
    probs_low = probs.astype(jnp.bfloat16)
    attended = jnp.dot(probs_low, head_v, preferred_element_type=jnp.float32)
    delta = lax.optimization_barrier(jnp.sum(head_g.astype(jnp.float32) * attended, axis=-1, keepdims=True))
    dprobs = jnp.dot(head_g, head_v.T, preferred_element_type=jnp.float32)
    dscores = (probs * (dprobs - delta) * inv_root).astype(jnp.bfloat16)
    grad_q = jnp.dot(dscores, head_k, preferred_element_type=jnp.float32).astype(jnp.bfloat16)
    grad_k = jnp.dot(dscores.T, head_q, preferred_element_type=jnp.float32).astype(jnp.bfloat16)
    grad_v = jnp.dot(probs_low.T, head_g, preferred_element_type=jnp.float32).astype(jnp.bfloat16)
    return (grad_q, grad_k, grad_v)

def group_grads(group_q, group_k, group_v, group_g, group_seg):
    inv_root = 1.0 / math.sqrt(HD)
    matched = group_seg[:, None] == group_seg[None, :]

    def split_heads(array):
        return array.reshape(GROUP_ROWS, H, HD).transpose(1, 0, 2)

    def per_head(items):
        return head_grads(items[0], items[1], items[2], items[3], matched, inv_root)
    results = lax.map(per_head, (split_heads(group_q), split_heads(group_k), split_heads(group_v), split_heads(group_g)))
    return tuple((item.transpose(1, 0, 2).reshape(GROUP_ROWS, D) for item in results))

def reference(queries, key_states, value_states, out_grads, row_order, segment_ids):
    devices = N_DP * N_SEQ
    order_blocks = row_order.reshape(devices, TOK_DEV).astype(jnp.int32)

    def balance(array):
        blocks = array.reshape(devices, TOK_DEV, D)
        permuted = jnp.take_along_axis(blocks, order_blocks[:, :, None], axis=1)
        moved = permuted.reshape(N_DP, N_SEQ, N_DP, SLICE, D).transpose(2, 1, 0, 3, 4)
        return moved.reshape(N_DP, GROUP_ROWS, D)

    def per_group(items):
        return group_grads(items[0], items[1], items[2], items[3], items[4])
    results = lax.map(per_group, (balance(queries), balance(key_states), balance(value_states), balance(out_grads), segment_ids))

    def restore(array):
        moved = array.reshape(N_DP, N_SEQ, N_DP, SLICE, D).transpose(2, 1, 0, 3, 4).reshape(devices, TOK_DEV, D)
        placed = jax.vmap(lambda block, order: jnp.zeros_like(block).at[order].set(block))(moved, order_blocks)
        return placed.reshape(TOKENS, D)
    return (restore(results[0]), restore(results[1]), restore(results[2]))
```

```python
import functools
import math

import jax
import jax.numpy as jnp
from jax import lax
from jax.experimental import pallas as pl
from jax.experimental.pallas import tpu as pltpu
from jax.sharding import PartitionSpec as P

HD = 80
ROWS = 128
WIDTH = 1280
HALF = 640
SEQ = 16
GROUP = 2048
PAD = 128
MESH = pl.DeviceIdType.MESH
BIG = 1e30
INV_ROOT = 1.0 / math.sqrt(HD)
LOG2E_ROOT = INV_ROOT * math.log2(math.e)
TILE = 256
LOW, HIGH = 6, 10
BANDS = ((0, 3, 0, 5), (3, 5, 0, 8), (5, 8, 3, 8))
K, Q, G, V = 0, 1, 2, 3
GV, GQ, GK = 0, 1, 2
BF16 = jnp.bfloat16
F32 = jnp.float32


def dot_nn(a, b):
    return lax.dot_general(a, b, (((1,), (0,)), ((), ())), preferred_element_type=F32)


def dot_nt(a, b):
    return lax.dot_general(a, b, (((1,), (1,)), ((), ())), preferred_element_type=F32)


def identity(n):
    return (
        lax.broadcasted_iota(jnp.int32, (n, n), 0) == lax.broadcasted_iota(jnp.int32, (n, n), 1)
    ).astype(F32).astype(BF16)


def kernel(
    q_ref, k_ref, v_ref, g_ref, order_ref, seg_ref,
    gq_ref, gk_ref, gv_ref,
    send1, recv1, send2, recv2, send3, recv3, send4, recv4,
    rows_k, rows_v, extra, probs, score, order_t,
    s1, r1, s2, r2, s3, r3, s4, r4,
):
    dp = lax.axis_index("dp")
    seq = lax.axis_index("seq")
    y_lo = lax.div(seq, 8)
    z = lax.rem(seq, 8)
    core = lax.rem(dp, 2)
    x = lax.rem(lax.div(dp, 2), 4)
    y = lax.div(dp, 8) * 2 + y_lo

    def plane(k):
        pc = lax.rem(core + lax.rem(k, 2), 2)
        px = lax.rem(x + lax.rem(lax.div(k, 2), 4), 4)
        py = lax.rem(y + lax.div(k, 8), 4)
        return lax.div(py, 2) * 8 + px * 2 + pc, lax.rem(py, 2)

    def column(k):
        return lax.rem(z + k, 8)

    barrier = pltpu.get_barrier_semaphore()

    def greet_plane(k, c):
        pd, pyl = plane(k)
        pl.semaphore_signal(barrier, inc=1, device_id=(pd, pyl * 8 + z), device_id_type=MESH)
        return c

    lax.fori_loop(1, 32, greet_plane, 0)

    def greet_column(k, c):
        pl.semaphore_signal(
            barrier, inc=1, device_id=(dp, y_lo * 8 + column(k)), device_id_type=MESH
        )
        return c

    lax.fori_loop(1, 8, greet_column, 0)

    eye = identity(ROWS)
    onehot_t = (
        lax.broadcasted_iota(jnp.int32, (ROWS, ROWS), 0)
        == jnp.broadcast_to(order_ref[...], (ROWS, ROWS))
    ).astype(F32).astype(BF16)
    order_t[...] = onehot_t
    onehot = dot_nt(eye, onehot_t).astype(BF16)

    def permute(t, ref):
        for half in range(2):
            part = dot_nn(onehot, ref[:, half * HALF:(half + 1) * HALF])
            send1[t, half * 16:(half + 1) * 16] = part.reshape(16, 8, HALF).astype(BF16)

    def start1(t):
        own = y_lo * 16 + dp

        def one(k, c):
            pd, pyl = plane(k)
            pltpu.make_async_remote_copy(
                src_ref=send1.at[t, pyl * 16 + pd],
                dst_ref=recv1.at[t, own],
                send_sem=s1.at[t],
                recv_sem=r1.at[t],
                device_id=(pd, pyl * 8 + z),
                device_id_type=MESH,
            ).start()
            return c

        lax.fori_loop(1, 32, one, 0)
        pltpu.make_async_copy(send1.at[t, own], recv1.at[t, own], r1.at[t]).start()

    def start2(t):
        pltpu.make_async_copy(recv1.at[t], recv1.at[t], r1.at[t]).wait()
        for half in range(2):
            rows = recv1[t, half * 16:(half + 1) * 16].astype(F32).reshape(ROWS, HALF).astype(BF16)
            for c in range(5):
                part = dot_nt(eye, rows[:, c * 128:(c + 1) * 128]).astype(BF16)
                send2[t, half, c * 128:(c + 1) * 128] = part
        for half in range(2):
            for k in (1, 7, 2, 6, 3, 5, 4):
                pz = column(k)
                pltpu.make_async_remote_copy(
                    src_ref=send2.at[t, half, pl.ds(pl.multiple_of(pz * HD, 16), HD)],
                    dst_ref=recv2.at[t, half * 8 + z],
                    send_sem=s2.at[t],
                    recv_sem=r2.at[t],
                    device_id=(dp, y_lo * 8 + pz),
                    device_id_type=MESH,
                ).start()
            pltpu.make_async_copy(
                send2.at[t, half, pl.ds(pl.multiple_of(z * HD, 16), HD)],
                recv2.at[t, half * 8 + z],
                r2.at[t],
            ).start()

    def arrived2(t):
        pltpu.make_async_copy(recv2.at[t], recv2.at[t], r2.at[t]).wait()

    def wide(t, first, last):
        return jnp.concatenate([recv2[t, s] for s in range(first, last)], axis=1)

    permute(K, k_ref)
    pl.semaphore_wait(barrier, 38)
    start1(K)
    permute(Q, q_ref)
    start1(Q)
    permute(G, g_ref)
    permute(V, v_ref)

    index = lax.broadcasted_iota(jnp.int32, (PAD - HD, GROUP), 0)
    seg = jnp.broadcast_to(seg_ref[...].astype(F32), (PAD - HD, GROUP))
    first, second = index == 0, index == 1
    extra[0] = jnp.where(first, seg, jnp.where(second, 1.0 - seg, 0.0)).astype(BF16)
    extra[1] = jnp.where(first, -BIG * (1.0 - seg), jnp.where(second, -BIG * seg, 0.0)).astype(BF16)

    start2(K)
    start1(G)
    start2(Q)
    start1(V)
    start2(G)

    arrived2(K)
    for s in range(SEQ):
        full = jnp.concatenate([recv2[K, s], extra[0, :, s * ROWS:(s + 1) * ROWS]], axis=0)
        rows_k[s * ROWS:(s + 1) * ROWS] = dot_nt(eye, full).astype(BF16)
    start2(V)
    arrived2(Q)

    for q_first, q_last, k_first, k_last in BANDS:

        def soft_tile(qt, c, k_first=k_first, k_last=k_last):
            lanes = pl.ds(pl.multiple_of(qt * TILE, TILE), TILE)
            q_t = jnp.concatenate(
                [
                    jnp.concatenate([recv2[Q, 2 * qt], recv2[Q, 2 * qt + 1]], axis=1),
                    extra[1, :, lanes],
                ],
                axis=0,
            )
            top = jnp.full((8, TILE), -jnp.inf, F32)
            for kt in range(k_first, k_last):
                part = dot_nn(rows_k[kt * TILE:(kt + 1) * TILE], q_t)
                score[kt * TILE:(kt + 1) * TILE] = part
                top = jnp.maximum(top, jnp.max(part.reshape(TILE // 8, 8, TILE), axis=0))
            top = jnp.max(top, axis=0, keepdims=True) * LOG2E_ROOT
            total = jnp.zeros((8, TILE), F32)
            for kt in range(k_first, k_last):
                part = jnp.exp2(score[kt * TILE:(kt + 1) * TILE] * LOG2E_ROOT - top)
                score[kt * TILE:(kt + 1) * TILE] = part
                total = total + jnp.sum(part.reshape(TILE // 8, 8, TILE), axis=0)
            scale = 1.0 / jnp.sum(total, axis=0, keepdims=True)
            for kt in range(k_first, k_last):
                probs[kt * TILE:(kt + 1) * TILE, lanes] = (
                    score[kt * TILE:(kt + 1) * TILE] * scale
                ).astype(BF16)
            return c

        lax.fori_loop(q_first, q_last, soft_tile, 0)

    def start3(t, s, unroll_z=None):
        pz = lax.rem(s, 8)
        half = lax.div(s, 8)

        @pl.when(pz != z)
        def _():
            pltpu.make_async_remote_copy(
                src_ref=send3.at[t, s],
                dst_ref=recv3.at[t, half, pl.ds(pl.multiple_of(z * HD, 16), HD)],
                send_sem=s3.at[t],
                recv_sem=r3.at[t],
                device_id=(dp, y_lo * 8 + pz),
                device_id_type=MESH,
            ).start()

        @pl.when(pz == z)
        def _():
            pltpu.make_async_copy(
                send3.at[t, s],
                recv3.at[t, half, pl.ds(pl.multiple_of(z * HD, 16), HD)],
                r3.at[t],
            ).start()

    def key_side(t, source, scale):
        for k_first, k_last, q_first, q_last in BANDS:
            left = wide(source, 2 * q_first, 2 * q_last)
            for kt in range(k_first, k_last):
                part = dot_nt(
                    left, probs[kt * TILE:(kt + 1) * TILE, q_first * TILE:q_last * TILE]
                )
                part = (part * scale).astype(BF16)
                send3[t, 2 * kt] = part[:, :ROWS]
                send3[t, 2 * kt + 1] = part[:, ROWS:]

    def start3_all(t):
        def one(i, c):
            start3(t, lax.rem(lax.div(i, 2) + z + 1, 8) + 8 * lax.rem(i, 2))
            return c

        lax.fori_loop(0, SEQ, one, 0)

    arrived2(G)
    key_side(GV, G, 1.0)
    start3_all(GV)

    arrived2(V)
    for s in range(SEQ):
        full = jnp.concatenate([recv2[V, s], jnp.zeros((PAD - HD, ROWS), BF16)], axis=0)
        rows_v[s * ROWS:(s + 1) * ROWS] = dot_nt(eye, full).astype(BF16)

    for q_first, q_last, k_first, k_last in BANDS:
        k_wide = wide(K, 2 * k_first, 2 * k_last)

        def grad_tile(qt, c, k_first=k_first, k_last=k_last, k_wide=k_wide):
            lanes = pl.ds(pl.multiple_of(qt * TILE, TILE), TILE)
            g_t = jnp.concatenate(
                [
                    jnp.concatenate([recv2[G, 2 * qt], recv2[G, 2 * qt + 1]], axis=1),
                    jnp.zeros((PAD - HD, TILE), BF16),
                ],
                axis=0,
            )
            delta = jnp.zeros((8, TILE), F32)
            for kt in range(k_first, k_last):
                part = dot_nn(rows_v[kt * TILE:(kt + 1) * TILE], g_t)
                score[kt * TILE:(kt + 1) * TILE] = part
                weighed = part * probs[kt * TILE:(kt + 1) * TILE, lanes].astype(F32)
                delta = delta + jnp.sum(weighed.reshape(TILE // 8, 8, TILE), axis=0)
            delta = jnp.sum(delta, axis=0, keepdims=True)
            for kt in range(k_first, k_last):
                part = score[kt * TILE:(kt + 1) * TILE] - delta
                part = part * probs[kt * TILE:(kt + 1) * TILE, lanes].astype(F32)
                probs[kt * TILE:(kt + 1) * TILE, lanes] = part.astype(BF16)
            grad = dot_nn(k_wide, probs[k_first * TILE:k_last * TILE, lanes]) * INV_ROOT
            grad = grad.astype(BF16)
            send3[GQ, 2 * qt] = grad[:, :ROWS]
            send3[GQ, 2 * qt + 1] = grad[:, ROWS:]
            return c

        lax.fori_loop(q_first, q_last, grad_tile, 0)

    start3_all(GQ)
    key_side(GK, Q, INV_ROOT)
    start3_all(GK)

    def start4(t):
        pltpu.make_async_copy(recv3.at[t], recv3.at[t], r3.at[t]).wait()
        own = y_lo * 16 + dp
        for half in range(2):
            for c in range(5):
                part = dot_nt(eye, recv3[t, half, c * 128:(c + 1) * 128])
                send4[t, half * 16:(half + 1) * 16, :, c * 128:(c + 1) * 128] = part.reshape(
                    16, 8, 128
                ).astype(BF16)

        def one(k, c):
            pd, pyl = plane(k)
            pltpu.make_async_remote_copy(
                src_ref=send4.at[t, pyl * 16 + pd],
                dst_ref=recv4.at[t, own],
                send_sem=s4.at[t],
                recv_sem=r4.at[t],
                device_id=(pd, pyl * 8 + z),
                device_id_type=MESH,
            ).start()
            return c

        lax.fori_loop(1, 32, one, 0)
        pltpu.make_async_copy(send4.at[t, own], recv4.at[t, own], r4.at[t]).start()

    def finish(t, ref):
        pltpu.make_async_copy(recv4.at[t], recv4.at[t], r4.at[t]).wait()
        for half in range(2):
            rows = recv4[t, half * 16:(half + 1) * 16].astype(F32).reshape(ROWS, HALF).astype(BF16)
            ref[:, half * HALF:(half + 1) * HALF] = dot_nn(order_t[...], rows).astype(BF16)

    start4(GV)
    start4(GQ)
    finish(GV, gv_ref)
    start4(GK)
    finish(GQ, gq_ref)
    finish(GK, gk_ref)

    for t in range(4):
        pltpu.make_async_copy(
            send1.at[t, pl.ds(0, 31)], send1.at[t, pl.ds(0, 31)], s1.at[t]
        ).wait()
        pltpu.make_async_copy(
            recv2.at[t, pl.ds(0, 14)], recv2.at[t, pl.ds(0, 14)], s2.at[t]
        ).wait()
    for t in range(3):
        pltpu.make_async_copy(
            send3.at[t, pl.ds(0, 14)], send3.at[t, pl.ds(0, 14)], s3.at[t]
        ).wait()
        pltpu.make_async_copy(
            send4.at[t, pl.ds(0, 31)], send4.at[t, pl.ds(0, 31)], s4.at[t]
        ).wait()


def on_device(queries, key_states, value_states, out_grads, row_order, segment_ids):
    out = jax.ShapeDtypeStruct((ROWS, WIDTH), BF16)
    vmem = pl.BlockSpec(memory_space=pltpu.VMEM)
    grads = pl.pallas_call(
        kernel,
        out_shape=(out, out, out),
        in_specs=[vmem] * 6,
        out_specs=(vmem, vmem, vmem),
        scratch_shapes=[
            pltpu.VMEM((4, 32, 8, HALF), BF16),
            pltpu.VMEM((4, 32, 8, HALF), BF16),
            pltpu.VMEM((4, 2, HALF, ROWS), BF16),
            pltpu.VMEM((4, SEQ, HD, ROWS), BF16),
            pltpu.VMEM((3, SEQ, HD, ROWS), BF16),
            pltpu.VMEM((3, 2, HALF, ROWS), BF16),
            pltpu.VMEM((3, 32, 8, HALF), BF16),
            pltpu.VMEM((3, 32, 8, HALF), BF16),
            pltpu.VMEM((GROUP, PAD), BF16),
            pltpu.VMEM((GROUP, PAD), BF16),
            pltpu.VMEM((2, PAD - HD, GROUP), BF16),
            pltpu.VMEM((GROUP, GROUP), BF16),
            pltpu.VMEM((GROUP, TILE), F32),
            pltpu.VMEM((ROWS, ROWS), BF16),
            pltpu.SemaphoreType.DMA((4,)),
            pltpu.SemaphoreType.DMA((4,)),
            pltpu.SemaphoreType.DMA((4,)),
            pltpu.SemaphoreType.DMA((4,)),
            pltpu.SemaphoreType.DMA((3,)),
            pltpu.SemaphoreType.DMA((3,)),
            pltpu.SemaphoreType.DMA((3,)),
            pltpu.SemaphoreType.DMA((3,)),
        ],
        compiler_params=pltpu.CompilerParams(collective_id=0, has_side_effects=True),
    )(queries, key_states, value_states, out_grads, row_order[None, :], segment_ids)
    return grads


def solution(mesh):
    rows = P(("dp", "seq"), None)
    return jax.shard_map(
        on_device,
        mesh=mesh,
        in_specs=(rows, rows, rows, rows, P(("dp", "seq")), P("dp", None)),
        out_specs=(rows, rows, rows),
        check_vma=False,
    )
```

```python
import functools
import math

import jax
import jax.numpy as jnp
from jax import lax
from jax.experimental import pallas as pl
from jax.experimental.pallas import tpu as pltpu
from jax.sharding import PartitionSpec as P

HD = 80
ROWS = 128
WIDTH = 1280
HALF = 640
SEQ = 16
GROUP = 2048
PAD = 128
MESH = pl.DeviceIdType.MESH
BIG = 1e30
INV_ROOT = 1.0 / math.sqrt(HD)
LOG2E_ROOT = INV_ROOT * math.log2(math.e)
TILE = 256
LOW, HIGH = 6, 10
BANDS = ((0, 3, 0, 5), (3, 5, 0, 8), (5, 8, 3, 8))
K, Q, G, V = 0, 1, 2, 3
GV, GQ, GK = 0, 1, 2
BF16 = jnp.bfloat16
F32 = jnp.float32


def dot_nn(a, b):
    return lax.dot_general(a, b, (((1,), (0,)), ((), ())), preferred_element_type=F32)


def dot_nt(a, b):
    return lax.dot_general(a, b, (((1,), (1,)), ((), ())), preferred_element_type=F32)


def identity(n):
    return (
        lax.broadcasted_iota(jnp.int32, (n, n), 0) == lax.broadcasted_iota(jnp.int32, (n, n), 1)
    ).astype(F32).astype(BF16)


def scope(name):
    return jax.named_scope(name)


def onehot_of(order_row):
    return (
        lax.broadcasted_iota(jnp.int32, (ROWS, ROWS), 0)
        == jnp.broadcast_to(order_row, (ROWS, ROWS))
    ).astype(F32).astype(BF16)


def put_back(onehot_t, blocks, ref):
    for half in range(2):
        rows = blocks[half].astype(F32).reshape(ROWS, HALF).astype(BF16)
        ref[:, half * HALF:(half + 1) * HALF] = dot_nn(onehot_t, rows).astype(BF16)


def kernel(
    q_hbm, k_hbm, v_hbm, g_hbm, order_hbm, seg_hbm,
    gv_ref, gq_ref, raw_ref,
    held, order_ref, seg_ref,
    send1, recv1, send2, recv2, send3, recv3, send4, recv4,
    rows_k, rows_v, extra, probs, score, order_t,
    load, s1, r1, s2, r2, s3, r3, s4, r4,
):
    dp = lax.axis_index("dp")
    seq = lax.axis_index("seq")
    y_lo = lax.div(seq, 8)
    z = lax.rem(seq, 8)
    core = lax.rem(dp, 2)
    x = lax.rem(lax.div(dp, 2), 4)
    y_hi = lax.div(dp, 8)
    other = 1 - y_lo

    def near(k):
        pc = lax.rem(core + lax.div(k, 8), 2)
        px = lax.rem(x + lax.rem(lax.div(k, 2), 4), 4)
        return lax.rem(y_hi + lax.rem(k, 2), 2) * 8 + px * 2 + pc

    def column(k):
        return lax.rem(z + k, 8)

    barrier = pltpu.get_barrier_semaphore()

    def greet(device):
        pl.semaphore_signal(barrier, inc=1, device_id=device, device_id_type=MESH)

    def greet_plane(k, c):
        pd = near(k)
        greet((pd, other * 8 + z))

        @pl.when(k > 0)
        def _():
            greet((pd, seq))

        return c

    def greet_column(k, c):
        greet((dp, y_lo * 8 + column(k)))
        return c

    loads = [
        pltpu.make_async_copy(src, dst, load.at[i])
        for i, (src, dst) in enumerate(
            [(order_hbm, order_ref)]
            + [(ref, held.at[t]) for t, ref in enumerate((k_hbm, q_hbm, g_hbm, v_hbm))]
            + [(seg_hbm, seg_ref)]
        )
    ]
    for copy in loads:
        copy.start()
    with scope("A_greet"):
        lax.fori_loop(1, 8, greet_column, 0)
        lax.fori_loop(0, 16, greet_plane, 0)

    eye = identity(ROWS)

    def permute(t, onehot):
        loads[1 + t].wait()
        for half in range(2):
            part = dot_nn(onehot, held[t, :, half * HALF:(half + 1) * HALF])
            send1[t, half] = part.reshape(16, 8, HALF).astype(BF16)

    def start1(t, half_is_other):
        half = other if half_is_other else y_lo

        def one(k, c):
            pd = near(k)
            pltpu.make_async_remote_copy(
                src_ref=send1.at[t, half, pd],
                dst_ref=recv1.at[t, y_lo, dp],
                send_sem=s1.at[t],
                recv_sem=r1.at[t, 0 if half_is_other else 1],
                device_id=(pd, half * 8 + z),
                device_id_type=MESH,
            ).start()
            return c

        lax.fori_loop(0 if half_is_other else 1, 16, one, 0)
        if not half_is_other:
            pltpu.make_async_copy(
                send1.at[t, half, dp], recv1.at[t, half, dp], r1.at[t, 1]
            ).start()

    def start2(t, half_is_other):
        half = other if half_is_other else y_lo
        with scope("wait1"):
            pltpu.make_async_copy(
                recv1.at[t, half], recv1.at[t, half], r1.at[t, 0 if half_is_other else 1]
            ).wait()
        rows = recv1[t, half].astype(F32).reshape(ROWS, HALF).astype(BF16)
        for c in range(5):
            part = dot_nt(eye, rows[:, c * 128:(c + 1) * 128]).astype(BF16)
            send2[t, half, c * 128:(c + 1) * 128] = part
        for k in (1, 7, 2, 6, 3, 5, 4):
            pz = column(k)
            pltpu.make_async_remote_copy(
                src_ref=send2.at[t, half, pl.ds(pl.multiple_of(pz * HD, 16), HD)],
                dst_ref=recv2.at[t, half * 8 + z],
                send_sem=s2.at[t],
                recv_sem=r2.at[t],
                device_id=(dp, y_lo * 8 + pz),
                device_id_type=MESH,
            ).start()
        pltpu.make_async_copy(
            send2.at[t, half, pl.ds(pl.multiple_of(z * HD, 16), HD)],
            recv2.at[t, half * 8 + z],
            r2.at[t],
        ).start()

    def arrived2(t):
        with scope("wait2"):
            pltpu.make_async_copy(recv2.at[t], recv2.at[t], r2.at[t]).wait()

    def wide(t, first, last):
        return jnp.concatenate([recv2[t, s] for s in range(first, last)], axis=1)

    with scope("A_perm"):
        loads[0].wait()
        onehot_t = onehot_of(order_ref[...])
        order_t[...] = onehot_t
        onehot = dot_nt(eye, onehot_t).astype(BF16)
        for t in (K, Q, G, V):
            permute(t, onehot)

    with scope("A_extra"):
        loads[5].wait()
        index = lax.broadcasted_iota(jnp.int32, (PAD - HD, GROUP), 0)
        seg = jnp.broadcast_to(seg_ref[...].astype(F32), (PAD - HD, GROUP))
        first, second = index == 0, index == 1
        extra[0] = jnp.where(first, seg, jnp.where(second, 1.0 - seg, 0.0)).astype(BF16)
        extra[1] = jnp.where(
            first, -BIG * (1.0 - seg), jnp.where(second, -BIG * seg, 0.0)
        ).astype(BF16)

    with scope("A_barrier"):
        pl.semaphore_wait(barrier, 38)
    with scope("A_start1K"):
        start1(K, True)
        start1(K, False)
    with scope("B_start2K"):
        start2(K, True)
    with scope("A_start1Q"):
        start1(Q, True)
        start1(Q, False)
    with scope("B_start2K"):
        start2(K, False)
    with scope("B_start2Q"):
        start2(Q, True)
    with scope("B_start1G"):
        start1(G, True)
        start1(G, False)
    with scope("B_start2Q"):
        start2(Q, False)
    with scope("B_start1V"):
        start1(V, True)
        start1(V, False)
    with scope("B_start2G"):
        start2(G, True)
        start2(G, False)

    arrived2(K)
    for s in range(SEQ):
        full = jnp.concatenate([recv2[K, s], extra[0, :, s * ROWS:(s + 1) * ROWS]], axis=0)
        rows_k[s * ROWS:(s + 1) * ROWS] = dot_nt(eye, full).astype(BF16)
    with scope("B_start2V"):
        start2(V, True)
        start2(V, False)
    arrived2(Q)

    for q_first, q_last, k_first, k_last in BANDS:

        def soft_tile(qt, c, k_first=k_first, k_last=k_last):
            lanes = pl.ds(pl.multiple_of(qt * TILE, TILE), TILE)
            q_t = jnp.concatenate(
                [
                    jnp.concatenate([recv2[Q, 2 * qt], recv2[Q, 2 * qt + 1]], axis=1),
                    extra[1, :, lanes],
                ],
                axis=0,
            )
            top = jnp.full((8, TILE), -jnp.inf, F32)
            for kt in range(k_first, k_last):
                part = dot_nn(rows_k[kt * TILE:(kt + 1) * TILE], q_t)
                score[kt * TILE:(kt + 1) * TILE] = part
                top = jnp.maximum(top, jnp.max(part.reshape(TILE // 8, 8, TILE), axis=0))
            top = jnp.max(top, axis=0, keepdims=True) * LOG2E_ROOT
            total = jnp.zeros((8, TILE), F32)
            for kt in range(k_first, k_last):
                part = jnp.exp2(score[kt * TILE:(kt + 1) * TILE] * LOG2E_ROOT - top)
                score[kt * TILE:(kt + 1) * TILE] = part
                total = total + jnp.sum(part.reshape(TILE // 8, 8, TILE), axis=0)
            scale = 1.0 / jnp.sum(total, axis=0, keepdims=True)
            for kt in range(k_first, k_last):
                probs[kt * TILE:(kt + 1) * TILE, lanes] = (
                    score[kt * TILE:(kt + 1) * TILE] * scale
                ).astype(BF16)
            return c

        with scope("C_soft"):
            lax.fori_loop(q_first, q_last, soft_tile, 0)

    def start3(t, half, pz, which):
        s = half * 8 + pz
        dst = recv3.at[t, half, pl.ds(pl.multiple_of(z * HD, 16), HD)]

        @pl.when(pz != z)
        def _():
            pltpu.make_async_remote_copy(
                src_ref=send3.at[t, s],
                dst_ref=dst,
                send_sem=s3.at[t],
                recv_sem=r3.at[t, which],
                device_id=(dp, y_lo * 8 + pz),
                device_id_type=MESH,
            ).start()

        @pl.when(pz == z)
        def _():
            pltpu.make_async_copy(send3.at[t, s], dst, r3.at[t, which]).start()

    def key_side(t, source, scale):
        for k_first, k_last, q_first, q_last in BANDS:
            left = wide(source, 2 * q_first, 2 * q_last)
            for kt in range(k_first, k_last):
                part = dot_nt(
                    left, probs[kt * TILE:(kt + 1) * TILE, q_first * TILE:q_last * TILE]
                )
                part = (part * scale).astype(BF16)
                send3[t, 2 * kt] = part[:, :ROWS]
                send3[t, 2 * kt + 1] = part[:, ROWS:]

    def start3_all(t):
        for which, half in ((0, y_lo), (1, other)):

            def one(k, c, which=which, half=half):
                start3(t, half, column(k), which)
                return c

            lax.fori_loop(1, 9, one, 0)

    arrived2(G)
    with scope("C_gv"):
        key_side(GV, G, 1.0)
    with scope("C_start3"):
        start3_all(GV)

    arrived2(V)
    for s in range(SEQ):
        full = jnp.concatenate([recv2[V, s], jnp.zeros((PAD - HD, ROWS), BF16)], axis=0)
        rows_v[s * ROWS:(s + 1) * ROWS] = dot_nt(eye, full).astype(BF16)

    def grad_tile(qt, k_first, k_last):
        lanes = pl.ds(pl.multiple_of(qt * TILE, TILE), TILE)
        g_t = jnp.concatenate(
            [
                jnp.concatenate([recv2[G, 2 * qt], recv2[G, 2 * qt + 1]], axis=1),
                jnp.zeros((PAD - HD, TILE), BF16),
            ],
            axis=0,
        )
        delta = jnp.zeros((8, TILE), F32)
        for kt in range(k_first, k_last):
            part = dot_nn(rows_v[kt * TILE:(kt + 1) * TILE], g_t)
            score[kt * TILE:(kt + 1) * TILE] = part
            weighed = part * probs[kt * TILE:(kt + 1) * TILE, lanes].astype(F32)
            delta = delta + jnp.sum(weighed.reshape(TILE // 8, 8, TILE), axis=0)
        delta = jnp.sum(delta, axis=0, keepdims=True)
        for kt in range(k_first, k_last):
            part = score[kt * TILE:(kt + 1) * TILE] - delta
            part = part * probs[kt * TILE:(kt + 1) * TILE, lanes].astype(F32)
            probs[kt * TILE:(kt + 1) * TILE, lanes] = part.astype(BF16)
        k_wide = wide(K, 2 * k_first, 2 * k_last)
        grad = dot_nn(k_wide, probs[k_first * TILE:k_last * TILE, lanes]) * INV_ROOT
        grad = grad.astype(BF16)
        send3[GQ, 2 * qt] = grad[:, :ROWS]
        send3[GQ, 2 * qt + 1] = grad[:, ROWS:]

    def grad_step(i, c):
        pair = lax.rem(lax.div(z, 2) + 1 + lax.div(i, 2), 4)
        half = lax.rem(i, 2)
        qt = pair + 4 * half
        for q_first, q_last, k_first, k_last in BANDS:

            @pl.when(jnp.logical_and(qt >= q_first, qt < q_last))
            def _(k_first=k_first, k_last=k_last):
                grad_tile(qt, k_first, k_last)

        for j in range(2):
            for which, mine in ((0, half == y_lo), (1, half != y_lo)):

                @pl.when(mine)
                def _(j=j, which=which):
                    start3(GQ, half, 2 * pair + j, which)

        return c

    with scope("D_grad"):
        lax.fori_loop(0, 8, grad_step, 0)
    def start4(t, which):
        half = other if which else y_lo
        with scope("wait3"):
            pltpu.make_async_copy(
                recv3.at[t, half], recv3.at[t, half], r3.at[t, which]
            ).wait()
        for c in range(5):
            part = dot_nt(eye, recv3[t, half, c * 128:(c + 1) * 128])
            send4[t, half, :, :, c * 128:(c + 1) * 128] = part.reshape(16, 8, 128).astype(BF16)

        def one(k, c):
            pd = near(k)
            pltpu.make_async_remote_copy(
                src_ref=send4.at[t, half, pd],
                dst_ref=(raw_ref if t == GK else recv4.at[t]).at[y_lo, dp],
                send_sem=s4.at[t],
                recv_sem=r4.at[t],
                device_id=(pd, half * 8 + z),
                device_id_type=MESH,
            ).start()
            return c

        lax.fori_loop(0 if which else 1, 16, one, 0)
        if not which:
            pltpu.make_async_copy(
                send4.at[t, half, dp],
                (raw_ref if t == GK else recv4.at[t]).at[half, dp],
                r4.at[t],
            ).start()

    with scope("E_start4V"):
        start4(GV, 0)
        start4(GV, 1)
    with scope("D_gk"):
        key_side(GK, Q, INV_ROOT)
    start3_all(GK)

    def finish(t, ref):
        with scope("wait4"):
            pltpu.make_async_copy(recv4.at[t], recv4.at[t], r4.at[t]).wait()
        put_back(order_t[...], recv4[t], ref)

    with scope("E_start4Q"):
        start4(GQ, 0)
        start4(GQ, 1)
    with scope("E_start4K0"):
        start4(GK, 0)
    with scope("E_start4K1"):
        start4(GK, 1)
    with scope("E_finV"):
        finish(GV, gv_ref)
    with scope("E_finQ"):
        finish(GQ, gq_ref)

    with scope("E_sent"):
        for t in range(4):
            for half in range(2):
                part = send1.at[t, half, pl.ds(0, 16 - half)]
                pltpu.make_async_copy(part, part, s1.at[t]).wait()
            part = recv2.at[t, pl.ds(0, 14)]
            pltpu.make_async_copy(part, part, s2.at[t]).wait()
        for t in range(3):
            part = send3.at[t, pl.ds(0, 14)]
            pltpu.make_async_copy(part, part, s3.at[t]).wait()
            for half in range(2):
                part = send4.at[t, half, pl.ds(0, 16 - half)]
                pltpu.make_async_copy(part, part, s4.at[t]).wait()
    with scope("E_last"):
        pltpu.make_async_copy(raw_ref, raw_ref, r4.at[GK]).wait()


def last_kernel(gv_ref, gq_ref, raw_ref, order_ref, gq_out, gk_out, gv_out):
    put_back(onehot_of(order_ref[...]), raw_ref[...], gk_out)
    gv_out[...] = gv_ref[...]
    gq_out[...] = gq_ref[...]


def on_device(queries, key_states, value_states, out_grads, row_order, segment_ids):
    out = jax.ShapeDtypeStruct((ROWS, WIDTH), BF16)
    raw = jax.ShapeDtypeStruct((2, 16, 8, HALF), BF16)
    vmem = pl.BlockSpec(memory_space=pltpu.VMEM)
    anywhere = pl.BlockSpec(memory_space=pl.ANY)
    order = row_order[None, :]
    parts = pl.pallas_call(
        kernel,
        out_shape=(out, out, raw),
        in_specs=[anywhere] * 6,
        out_specs=(vmem, vmem, vmem),
        scratch_shapes=[
            pltpu.VMEM((4, ROWS, WIDTH), BF16),
            pltpu.VMEM((1, ROWS), jnp.int32),
            pltpu.VMEM((1, GROUP), jnp.int32),
            pltpu.VMEM((4, 2, 16, 8, HALF), BF16),
            pltpu.VMEM((4, 2, 16, 8, HALF), BF16),
            pltpu.VMEM((4, 2, HALF, ROWS), BF16),
            pltpu.VMEM((4, SEQ, HD, ROWS), BF16),
            pltpu.VMEM((3, SEQ, HD, ROWS), BF16),
            pltpu.VMEM((3, 2, HALF, ROWS), BF16),
            pltpu.VMEM((3, 2, 16, 8, HALF), BF16),
            pltpu.VMEM((2, 2, 16, 8, HALF), BF16),
            pltpu.VMEM((GROUP, PAD), BF16),
            pltpu.VMEM((GROUP, PAD), BF16),
            pltpu.VMEM((2, PAD - HD, GROUP), BF16),
            pltpu.VMEM((GROUP, GROUP), BF16),
            pltpu.VMEM((GROUP, TILE), F32),
            pltpu.VMEM((ROWS, ROWS), BF16),
            pltpu.SemaphoreType.DMA((6,)),
            pltpu.SemaphoreType.DMA((4,)),
            pltpu.SemaphoreType.DMA((4, 2)),
            pltpu.SemaphoreType.DMA((4,)),
            pltpu.SemaphoreType.DMA((4,)),
            pltpu.SemaphoreType.DMA((3,)),
            pltpu.SemaphoreType.DMA((3, 2)),
            pltpu.SemaphoreType.DMA((3,)),
            pltpu.SemaphoreType.DMA((3,)),
        ],
        compiler_params=pltpu.CompilerParams(collective_id=0, has_side_effects=True),
    )(queries, key_states, value_states, out_grads, order, segment_ids)
    return pl.pallas_call(
        last_kernel,
        out_shape=(out, out, out),
        in_specs=[vmem] * 4,
        out_specs=(vmem, vmem, vmem),
    )(*parts, order)


def solution(mesh):
    rows = P(("dp", "seq"), None)
    return jax.shard_map(
        on_device,
        mesh=mesh,
        in_specs=(rows, rows, rows, rows, P(("dp", "seq")), P("dp", None)),
        out_specs=(rows, rows, rows),
        check_vma=False,
    )
```

```python
import functools
import math

import jax
import jax.numpy as jnp
from jax import lax
from jax.experimental import pallas as pl
from jax.experimental.pallas import tpu as pltpu
from jax.sharding import PartitionSpec as P

HD = 80
ROWS = 128
WIDTH = 1280
HALF = 640
SEQ = 16
GROUP = 2048
PAD = 128
MESH = pl.DeviceIdType.MESH
BIG = 1e30
INV_ROOT = 1.0 / math.sqrt(HD)
LOG2E_ROOT = INV_ROOT * math.log2(math.e)
TILE = 256
LOW, HIGH = 6, 10
BANDS = ((0, 3, 0, 5), (3, 5, 0, 8), (5, 8, 3, 8))
K, Q, G, V = 0, 1, 2, 3
GV, GQ, GK = 0, 1, 2
FAR_FIRST = sorted(range(16), key=lambda k: -(k % 2 + (0, 1, 2, 1)[k // 2 % 4]))
BF16 = jnp.bfloat16
F32 = jnp.float32


def dot_nn(a, b):
    return lax.dot_general(a, b, (((1,), (0,)), ((), ())), preferred_element_type=F32)


def dot_nt(a, b):
    return lax.dot_general(a, b, (((1,), (1,)), ((), ())), preferred_element_type=F32)


def identity(n):
    return (
        lax.broadcasted_iota(jnp.int32, (n, n), 0) == lax.broadcasted_iota(jnp.int32, (n, n), 1)
    ).astype(F32).astype(BF16)


def scope(name):
    return jax.named_scope(name)


def onehot_of(order_row):
    return (
        lax.broadcasted_iota(jnp.int32, (ROWS, ROWS), 0)
        == jnp.broadcast_to(order_row, (ROWS, ROWS))
    ).astype(F32).astype(BF16)


def kernel(
    q_hbm, k_hbm, v_hbm, g_hbm, order_hbm, seg_hbm,
    gv_ref, gq_ref, raw_ref, order_t,
    held, order_ref, seg_ref, eye_ref,
    sendz, recvz, send1, recv1, send2, recv2, keys_t,
    send3, recv3, send4, recv4, grad_k, send5, recv5, send6,
    rows_k, rows_v, extra, probs, score,
    load, s0, r0, s1, r1, s2, r2, s3, r3, s4, r4, s5, r5, s6, r6,
):
    dp = lax.axis_index("dp")
    seq = lax.axis_index("seq")
    y_lo = lax.div(seq, 8)
    z = lax.rem(seq, 8)
    core = lax.rem(dp, 2)
    x = lax.rem(lax.div(dp, 2), 4)
    y_hi = lax.div(dp, 8)
    other = 1 - y_lo

    def near(k):
        pc = lax.rem(core + k // 8, 2)
        px = lax.rem(x + k // 2 % 4, 4)
        return lax.rem(y_hi + k % 2, 2) * 8 + px * 2 + pc

    def column(k):
        return lax.rem(z + k, 8)

    def head_rows(k):
        return pl.ds(pl.multiple_of(k * HD, 16), HD)

    def arrive(ref, sem):
        pltpu.make_async_copy(ref, ref, sem).wait()

    barrier = pltpu.get_barrier_semaphore()

    def greet(device):
        pl.semaphore_signal(barrier, inc=1, device_id=device, device_id_type=MESH)

    loads = [
        pltpu.make_async_copy(src, dst, load.at[i])
        for i, (src, dst) in enumerate(
            [(order_hbm, order_ref)]
            + [(ref, held.at[t]) for t, ref in enumerate((k_hbm, q_hbm, g_hbm, v_hbm))]
            + [(seg_hbm, seg_ref)]
        )
    ]
    for copy in loads:
        copy.start()
    with scope("A_greet"):
        for k in (4, 3, 5, 2, 6, 1, 7):
            greet((dp, y_lo * 8 + column(k)))
        for k in FAR_FIRST:
            pd = near(k)
            greet((pd, other * 8 + z))
            if k:
                greet((pd, seq))

    eye_ref[...] = identity(ROWS)

    def to_rows(src, dst):
        for c in range(5):
            part = dot_nt(eye_ref[...], src[c * 128:(c + 1) * 128])
            dst[:, :, c * 128:(c + 1) * 128] = part.reshape(16, 8, 128).astype(BF16)

    def to_columns(src, dst):
        rows = src[...].astype(F32).reshape(ROWS, HALF).astype(BF16)
        for c in range(5):
            part = dot_nt(eye_ref[...], rows[:, c * 128:(c + 1) * 128])
            dst[c * 128:(c + 1) * 128] = part.astype(BF16)

    def plane_send(src, dst, half, send_sem, recv_sem):
        for k in FAR_FIRST:
            pd = near(k)

            def remote(pd=pd):
                pltpu.make_async_remote_copy(
                    src_ref=src.at[pd],
                    dst_ref=dst.at[y_lo, dp],
                    send_sem=send_sem,
                    recv_sem=recv_sem.at[y_lo],
                    device_id=(pd, half * 8 + z),
                    device_id_type=MESH,
                ).start()

            def local():
                pltpu.make_async_copy(
                    src.at[dp], dst.at[y_lo, dp], recv_sem.at[y_lo]
                ).start()

            if k:
                remote()
            else:
                pl.when(half != y_lo)(remote)
                pl.when(half == y_lo)(local)

    def column_send(src, dst, send_sem, recv_sem):
        for k in (4, 3, 5, 2, 6, 1, 7):
            pz = column(k)
            pltpu.make_async_remote_copy(
                src_ref=src.at[head_rows(pz)],
                dst_ref=dst,
                send_sem=send_sem,
                recv_sem=recv_sem,
                device_id=(dp, y_lo * 8 + pz),
                device_id_type=MESH,
            ).start()
        pltpu.make_async_copy(src.at[head_rows(z)], dst, recv_sem).start()

    def permuted(t, half, onehot):
        return dot_nn(onehot, held[t, :, half * HALF:(half + 1) * HALF])

    def permute(t, onehot):
        loads[1 + t].wait()
        for half in range(2):
            send1[t, half] = permuted(t, half, onehot).reshape(16, 8, HALF).astype(BF16)

    def start1(t):
        for half in (other, y_lo):
            plane_send(send1.at[t, half], recv1.at[t], half, s1.at[t], r1.at[t])

    def start2(t):
        for half in (other, y_lo):
            with scope("wait1"):
                arrive(recv1.at[t, half], r1.at[t, half])
            to_columns(recv1.at[t, half], send2.at[t, half])
            column_send(send2.at[t, half], recv2.at[t, half * 8 + z], s2.at[t], r2.at[t])

    def arrived2(t):
        with scope("wait2"):
            arrive(recv2.at[t], r2.at[t])

    def block(t, s):
        if t == K:
            return keys_t[s // 8, s % 8 * HD:(s % 8 + 1) * HD]
        return recv2[t, s]

    def wide(t, first, last):
        return jnp.concatenate([block(t, s) for s in range(first, last)], axis=1)

    with scope("A_permK"):
        loads[0].wait()
        onehot_t = onehot_of(order_ref[...])
        order_t[...] = onehot_t
        onehot = dot_nt(eye_ref[...], onehot_t).astype(BF16)
        loads[1 + K].wait()
        for half in range(2):
            rows = permuted(K, half, onehot).astype(BF16)
            for c in range(5):
                part = dot_nt(eye_ref[...], rows[:, c * 128:(c + 1) * 128])
                sendz[half, c * 128:(c + 1) * 128] = part.astype(BF16)
    with scope("A_permQ"):
        permute(Q, onehot)
    with scope("A_barrier"):
        pl.semaphore_wait(barrier, 38)
    with scope("A_sendz"):
        for half in (other, y_lo):
            column_send(sendz.at[half], recvz.at[half, head_rows(z)], s0, r0.at[half])
    with scope("A_start1Q"):
        start1(Q)
    with scope("A_permGV"):
        permute(G, onehot)
    with scope("B_start1G"):
        start1(G)
    with scope("A_permGV"):
        permute(V, onehot)
        loads[5].wait()
        index = lax.broadcasted_iota(jnp.int32, (PAD - HD, GROUP), 0)
        seg = jnp.broadcast_to(seg_ref[...].astype(F32), (PAD - HD, GROUP))
        first, second = index == 0, index == 1
        extra[0] = jnp.where(first, seg, jnp.where(second, 1.0 - seg, 0.0)).astype(BF16)
        extra[1] = jnp.where(
            first, -BIG * (1.0 - seg), jnp.where(second, -BIG * seg, 0.0)
        ).astype(BF16)

    def keys_on(half):
        with scope("wait0"):
            arrive(recvz.at[half], r0.at[half])
        to_rows(recvz.at[half], send1.at[K, half])
        plane_send(send1.at[K, half], recv1.at[K], half, s1.at[K], r1.at[K])

    with scope("B_start2Q"):
        start2(Q)
    with scope("B_keysA"):
        keys_on(other)
    with scope("B_keysB"):
        keys_on(y_lo)
    with scope("B_start1V"):
        start1(V)
    with scope("B_start2G"):
        start2(G)

    with scope("B_keysin"):
        for half in range(2):
            with scope("waitK"):
                arrive(recv1.at[K, half], r1.at[K, half])
            to_columns(recv1.at[K, half], keys_t.at[half])
        for s in range(SEQ):
            full = jnp.concatenate([block(K, s), extra[0, :, s * ROWS:(s + 1) * ROWS]], axis=0)
            rows_k[s * ROWS:(s + 1) * ROWS] = dot_nt(eye_ref[...], full).astype(BF16)
    arrived2(Q)

    def pair_of(t, qt):
        return jnp.concatenate([recv2[t, 2 * qt], recv2[t, 2 * qt + 1]], axis=1)

    for q_first, q_last, k_first, k_last in BANDS:

        def soft_tile(qt, c, k_first=k_first, k_last=k_last):
            lanes = pl.ds(pl.multiple_of(qt * TILE, TILE), TILE)
            q_t = jnp.concatenate([pair_of(Q, qt), extra[1, :, lanes]], axis=0)
            top = jnp.full((8, TILE), -jnp.inf, F32)
            for kt in range(k_first, k_last):
                part = dot_nn(rows_k[kt * TILE:(kt + 1) * TILE], q_t)
                score[kt * TILE:(kt + 1) * TILE] = part
                top = jnp.maximum(top, jnp.max(part.reshape(TILE // 8, 8, TILE), axis=0))
            top = jnp.max(top, axis=0, keepdims=True) * LOG2E_ROOT
            total = jnp.zeros((8, TILE), F32)
            for kt in range(k_first, k_last):
                part = jnp.exp2(score[kt * TILE:(kt + 1) * TILE] * LOG2E_ROOT - top)
                score[kt * TILE:(kt + 1) * TILE] = part
                total = total + jnp.sum(part.reshape(TILE // 8, 8, TILE), axis=0)
            scale = 1.0 / jnp.sum(total, axis=0, keepdims=True)
            for kt in range(k_first, k_last):
                probs[kt * TILE:(kt + 1) * TILE, lanes] = (
                    score[kt * TILE:(kt + 1) * TILE] * scale
                ).astype(BF16)
            return c

        with scope("C_soft"):
            lax.fori_loop(q_first, q_last, soft_tile, 0)
        if q_first == 0:
            with scope("B_start2V"):
                start2(V)

    def start3(t, half, pz):
        s = half * 8 + pz
        dst = recv3.at[t, half, head_rows(z)]

        @pl.when(pz != z)
        def _():
            pltpu.make_async_remote_copy(
                src_ref=send3.at[t, s],
                dst_ref=dst,
                send_sem=s3.at[t],
                recv_sem=r3.at[t, half],
                device_id=(dp, y_lo * 8 + pz),
                device_id_type=MESH,
            ).start()

        @pl.when(pz == z)
        def _():
            pltpu.make_async_copy(send3.at[t, s], dst, r3.at[t, half]).start()

    def key_side(source, band, done):
        k_first, k_last, q_first, q_last = band
        left = wide(source, 2 * q_first, 2 * q_last)
        for kt in range(k_first, k_last):
            done(
                kt,
                dot_nt(left, probs[kt * TILE:(kt + 1) * TILE, q_first * TILE:q_last * TILE]),
            )

    arrived2(G)
    with scope("C_gv"):

        def gv_done(kt, part):
            part = part.astype(BF16)
            send3[GV, 2 * kt] = part[:, :ROWS]
            send3[GV, 2 * kt + 1] = part[:, ROWS:]

        for band in BANDS:
            key_side(G, band, gv_done)
    with scope("C_start3"):
        for half in range(2):

            def one(k, c, half=half):
                start3(GV, half, column(k))
                return c

            lax.fori_loop(4, 12, one, 0)

    arrived2(V)
    tail = (lax.broadcasted_iota(jnp.int32, (PAD - HD, ROWS), 0) < 3).astype(F32).astype(BF16)
    for s in range(SEQ):
        full = jnp.concatenate([recv2[V, s], tail], axis=0)
        rows_v[s * ROWS:(s + 1) * ROWS] = dot_nt(eye_ref[...], full).astype(BF16)

    def grad_tile(qt, k_first, k_last):
        lanes = pl.ds(pl.multiple_of(qt * TILE, TILE), TILE)
        g_t = pair_of(G, qt)
        keys = slice(k_first * TILE, k_last * TILE)
        attended = dot_nn(wide(V, 2 * k_first, 2 * k_last), probs[keys, lanes])
        delta = -jnp.sum(g_t.astype(F32) * attended, axis=0, keepdims=True)
        high = delta.astype(BF16).astype(F32)
        middle = (delta - high).astype(BF16).astype(F32)
        low = delta - high - middle
        index = lax.broadcasted_iota(jnp.int32, (PAD - HD, TILE), 0)
        more = jnp.where(
            index == 0, high, jnp.where(index == 1, middle, jnp.where(index == 2, low, 0.0))
        ).astype(BF16)
        g_t = jnp.concatenate([g_t, more], axis=0)
        for kt in range(k_first, k_last):
            part = dot_nn(rows_v[kt * TILE:(kt + 1) * TILE], g_t)
            part = part * probs[kt * TILE:(kt + 1) * TILE, lanes].astype(F32)
            probs[kt * TILE:(kt + 1) * TILE, lanes] = part.astype(BF16)
        grad = dot_nn(wide(K, 2 * k_first, 2 * k_last), probs[keys, lanes]) * INV_ROOT
        grad = grad.astype(BF16)
        send3[GQ, 2 * qt] = grad[:, :ROWS]
        send3[GQ, 2 * qt + 1] = grad[:, ROWS:]

    def grad_step(i, c):
        pair = lax.rem(lax.div(z, 2) + 1 + lax.div(i, 2), 4)
        half = lax.rem(i, 2)
        qt = pair + 4 * half
        for q_first, q_last, k_first, k_last in BANDS:

            @pl.when(jnp.logical_and(qt >= q_first, qt < q_last))
            def _(k_first=k_first, k_last=k_last):
                grad_tile(qt, k_first, k_last)

        for j in range(2):
            start3(GQ, half, 2 * pair + j)
        return c

    with scope("D_grad"):
        lax.fori_loop(0, 8, grad_step, 0)

    with scope("D_gk"):

        def gk_done(kt, part):
            part = (part * INV_ROOT).astype(BF16)
            for j in range(2):
                s = 2 * kt + j
                grad_k[s // 8, s % 8 * HD:(s % 8 + 1) * HD] = part[:, j * ROWS:(j + 1) * ROWS]
            if kt % 4 == 3:
                half = kt // 4
                to_rows(grad_k.at[half], send5.at[half])
                plane_send(send5.at[half], recv5, half, s5, r5)

        for band in BANDS:
            key_side(Q, band, gk_done)

    def start4(t):
        for half in (y_lo, other):
            with scope("wait3"):
                arrive(recv3.at[t, half], r3.at[t, half])
            to_rows(recv3.at[t, half], send4.at[t, half])
            plane_send(send4.at[t, half], recv4.at[t], half, s4.at[t], r4.at[t])

    def finish(t, ref):
        for half in range(2):
            with scope("wait4"):
                arrive(recv4.at[t, half], r4.at[t, half])
            rows = recv4[t, half].astype(F32).reshape(ROWS, HALF).astype(BF16)
            held[t, :, half * HALF:(half + 1) * HALF] = dot_nn(order_t[...], rows).astype(BF16)
        pltpu.make_async_copy(held.at[t], ref, load.at[t]).start()

    with scope("E_start4V"):
        start4(GV)
    with scope("E_gk_on"):
        for half in (y_lo, other):
            with scope("wait5"):
                arrive(recv5.at[half], r5.at[half])
            to_columns(recv5.at[half], send6.at[half])
            column_send(send6.at[half], raw_ref.at[head_rows(half * 8 + z)], s6, r6)
    with scope("E_start4Q"):
        start4(GQ)
    with scope("E_finV"):
        finish(GV, gv_ref)
    with scope("E_finQ"):
        finish(GQ, gq_ref)

    with scope("E_sent"):
        def left(ref, sem):
            pltpu.make_async_copy(ref, ref, sem).wait()

        def plane_left(ref, sem):
            left(ref.at[0], sem)
            left(ref.at[1, pl.ds(0, 15)], sem)

        for t in range(4):
            plane_left(send1.at[t], s1.at[t])
        column_all = recv2.at[Q, pl.ds(0, 14)]
        left(column_all, s0)
        for t in (Q, G, V):
            left(column_all, s2.at[t])
        for t in range(2):
            left(column_all, s3.at[t])
            plane_left(send4.at[t], s4.at[t])
        plane_left(send5, s5)
        left(column_all, s6)
    with scope("E_last"):
        for t, ref in ((GV, gv_ref), (GQ, gq_ref)):
            pltpu.make_async_copy(held.at[t], ref, load.at[t]).wait()
        arrive(raw_ref, r6)


def last_kernel(gv_ref, gq_ref, raw_ref, order_t, gq_out, gk_out, gv_out):
    gk_out[...] = dot_nt(order_t[...], raw_ref[...]).astype(BF16)
    gv_out[...] = gv_ref[...]
    gq_out[...] = gq_ref[...]


def on_device(queries, key_states, value_states, out_grads, row_order, segment_ids):
    out = jax.ShapeDtypeStruct((ROWS, WIDTH), BF16)
    raw = jax.ShapeDtypeStruct((WIDTH, ROWS), BF16)
    vmem = pl.BlockSpec(memory_space=pltpu.VMEM)
    anywhere = pl.BlockSpec(memory_space=pl.ANY)
    order = row_order[None, :]
    rows_form = (2, 16, 8, HALF)
    columns_form = (2, HALF, ROWS)
    dma = pltpu.SemaphoreType.DMA
    inputs = (queries, key_states, value_states, out_grads, order, segment_ids)
    parts = pl.pallas_call(
        kernel,
        out_shape=(out, out, raw, jax.ShapeDtypeStruct((ROWS, ROWS), BF16)),
        in_specs=[pl.BlockSpec(memory_space=pltpu.HBM)] * 6,
        out_specs=(anywhere, anywhere, anywhere, vmem),
        scratch_shapes=[
            pltpu.VMEM((4, ROWS, WIDTH), BF16),
            pltpu.VMEM((1, ROWS), jnp.int32),
            pltpu.VMEM((1, GROUP), jnp.int32),
            pltpu.VMEM((ROWS, ROWS), BF16),
            pltpu.VMEM(columns_form, BF16),
            pltpu.VMEM(columns_form, BF16),
            pltpu.VMEM((4, *rows_form), BF16),
            pltpu.VMEM((4, *rows_form), BF16),
            pltpu.VMEM((4, *columns_form), BF16),
            pltpu.VMEM((4, SEQ, HD, ROWS), BF16),
            pltpu.VMEM(columns_form, BF16),
            pltpu.VMEM((2, SEQ, HD, ROWS), BF16),
            pltpu.VMEM((2, *columns_form), BF16),
            pltpu.VMEM((2, *rows_form), BF16),
            pltpu.VMEM((2, *rows_form), BF16),
            pltpu.VMEM(columns_form, BF16),
            pltpu.VMEM(rows_form, BF16),
            pltpu.VMEM(rows_form, BF16),
            pltpu.VMEM(columns_form, BF16),
            pltpu.VMEM((GROUP, PAD), BF16),
            pltpu.VMEM((GROUP, PAD), BF16),
            pltpu.VMEM((2, PAD - HD, GROUP), BF16),
            pltpu.VMEM((GROUP, GROUP), BF16),
            pltpu.VMEM((GROUP, TILE), F32),
            dma((6,)),
            dma, dma((2,)),
            dma((4,)), dma((4, 2)),
            dma((4,)), dma((4,)),
            dma((2,)), dma((2, 2)),
            dma((2,)), dma((2, 2)),
            dma, dma((2,)),
            dma, dma,
        ],
        compiler_params=pltpu.CompilerParams(
            collective_id=0, has_side_effects=True, vmem_limit_bytes=40 << 20
        ),
    )(*(pltpu.with_memory_space_constraint(a, pltpu.HBM) for a in inputs))
    return pl.pallas_call(
        last_kernel,
        out_shape=(out, out, out),
        in_specs=[vmem] * 4,
        out_specs=(vmem, vmem, vmem),
        compiler_params=pltpu.CompilerParams(vmem_limit_bytes=8 << 20),
    )(*parts)


def solution(mesh):
    rows = P(("dp", "seq"), None)
    return jax.shard_map(
        on_device,
        mesh=mesh,
        in_specs=(rows, rows, rows, rows, P(("dp", "seq")), P("dp", None)),
        out_specs=(rows, rows, rows),
        check_vma=False,
    )
```

```python
import functools
import math

import jax
import jax.numpy as jnp
from jax import lax
from jax.experimental import pallas as pl
from jax.experimental.pallas import tpu as pltpu
from jax.sharding import PartitionSpec as P

HD = 80
ROWS = 128
WIDTH = 1280
HALF = 640
SEQ = 16
GROUP = 2048
PAD = 128
MESH = pl.DeviceIdType.MESH
BIG = 1e30
INV_ROOT = 1.0 / math.sqrt(HD)
LOG2E_ROOT = INV_ROOT * math.log2(math.e)
TILE = 256
LOW, HIGH = 6, 10
BANDS = ((0, 3, 0, 5), (3, 5, 0, 8), (5, 8, 3, 8))
K, Q, G, V = 0, 1, 2, 3
GV, GK, GQ = 0, 1, 2
FAR_FIRST = sorted(range(16), key=lambda k: -(k % 2 + (0, 1, 2, 1)[k // 2 % 4]))
BF16 = jnp.bfloat16
F32 = jnp.float32


def dot_nn(a, b):
    return lax.dot_general(a, b, (((1,), (0,)), ((), ())), preferred_element_type=F32)


def dot_nt(a, b):
    return lax.dot_general(a, b, (((1,), (1,)), ((), ())), preferred_element_type=F32)


def identity(n):
    return (
        lax.broadcasted_iota(jnp.int32, (n, n), 0) == lax.broadcasted_iota(jnp.int32, (n, n), 1)
    ).astype(F32).astype(BF16)


def scope(name):
    return jax.named_scope(name)


def onehot_of(order_row):
    return (
        lax.broadcasted_iota(jnp.int32, (ROWS, ROWS), 0)
        == jnp.broadcast_to(order_row, (ROWS, ROWS))
    ).astype(F32).astype(BF16)


def kernel(
    q_hbm, k_hbm, v_hbm, g_hbm, order_hbm, seg_hbm,
    gv_ref, gk_ref, raw_ref, order_t,
    held, order_ref, seg_ref, eye_ref,
    sendz, recvz, send1, recv1, send2, recv2, keys_t,
    send3, recv3, send4, recv4, grad_q, send5, recv5, send6,
    rows_k, rows_v, extra, probs, score,
    load, s0, r0, s1, r1, s2, r2, s3, r3, s4, r4, s5, r5, s6, r6,
):
    dp = lax.axis_index("dp")
    seq = lax.axis_index("seq")
    y_lo = lax.div(seq, 8)
    z = lax.rem(seq, 8)
    core = lax.rem(dp, 2)
    x = lax.rem(lax.div(dp, 2), 4)
    y_hi = lax.div(dp, 8)
    other = 1 - y_lo

    def near(k):
        pc = lax.rem(core + k // 8, 2)
        px = lax.rem(x + k // 2 % 4, 4)
        return lax.rem(y_hi + k % 2, 2) * 8 + px * 2 + pc

    def column(k):
        return lax.rem(z + k, 8)

    def head_rows(k):
        return pl.ds(pl.multiple_of(k * HD, 16), HD)

    def arrive(ref, sem):
        pltpu.make_async_copy(ref, ref, sem).wait()

    barrier = pltpu.get_barrier_semaphore()

    def greet(device):
        pl.semaphore_signal(barrier, inc=1, device_id=device, device_id_type=MESH)

    loads = [
        pltpu.make_async_copy(src, dst, load.at[i])
        for i, (src, dst) in enumerate(
            [(order_hbm, order_ref)]
            + [(ref, held.at[t]) for t, ref in enumerate((k_hbm, q_hbm, g_hbm, v_hbm))]
            + [(seg_hbm, seg_ref)]
        )
    ]
    for copy in loads:
        copy.start()
    with scope("A_greet"):
        for k in (4, 3, 5, 2, 6, 1, 7):
            greet((dp, y_lo * 8 + column(k)))
        for k in FAR_FIRST:
            pd = near(k)
            greet((pd, other * 8 + z))
            if k:
                greet((pd, seq))

    eye_ref[...] = identity(ROWS)

    def to_rows(src, dst):
        for c in range(5):
            part = dot_nt(eye_ref[...], src[c * 128:(c + 1) * 128])
            dst[:, :, c * 128:(c + 1) * 128] = part.reshape(16, 8, 128).astype(BF16)

    def to_columns(src, dst):
        rows = src[...].astype(F32).reshape(ROWS, HALF).astype(BF16)
        for c in range(5):
            part = dot_nt(eye_ref[...], rows[:, c * 128:(c + 1) * 128])
            dst[c * 128:(c + 1) * 128] = part.astype(BF16)

    def plane_send(src, dst, half, send_sem, recv_sem):
        for k in FAR_FIRST:
            pd = near(k)

            def remote(pd=pd):
                pltpu.make_async_remote_copy(
                    src_ref=src.at[pd],
                    dst_ref=dst.at[y_lo, dp],
                    send_sem=send_sem,
                    recv_sem=recv_sem.at[y_lo],
                    device_id=(pd, half * 8 + z),
                    device_id_type=MESH,
                ).start()

            def local():
                pltpu.make_async_copy(
                    src.at[dp], dst.at[y_lo, dp], recv_sem.at[y_lo]
                ).start()

            if k:
                remote()
            else:
                pl.when(half != y_lo)(remote)
                pl.when(half == y_lo)(local)

    def column_send(src, dst, send_sem, recv_sem):
        for k in (4, 3, 5, 2, 6, 1, 7):
            pz = column(k)
            pltpu.make_async_remote_copy(
                src_ref=src.at[head_rows(pz)],
                dst_ref=dst,
                send_sem=send_sem,
                recv_sem=recv_sem,
                device_id=(dp, y_lo * 8 + pz),
                device_id_type=MESH,
            ).start()
        pltpu.make_async_copy(src.at[head_rows(z)], dst, recv_sem).start()

    def permuted(t, half, onehot):
        return dot_nn(onehot, held[t, :, half * HALF:(half + 1) * HALF])

    def permute(t, onehot):
        loads[1 + t].wait()
        for half in range(2):
            send1[t, half] = permuted(t, half, onehot).reshape(16, 8, HALF).astype(BF16)

    def start1(t):
        for half in (other, y_lo):
            plane_send(send1.at[t, half], recv1.at[t], half, s1.at[t], r1.at[t])

    def start2(t):
        for half in (other, y_lo):
            with scope("wait1"):
                arrive(recv1.at[t, half], r1.at[t, half])
            to_columns(recv1.at[t, half], send2.at[t, half])
            column_send(send2.at[t, half], recv2.at[t, half * 8 + z], s2.at[t], r2.at[t])

    def arrived2(t):
        with scope("wait2"):
            arrive(recv2.at[t], r2.at[t])

    def block(t, s):
        if t == K:
            return keys_t[s // 8, s % 8 * HD:(s % 8 + 1) * HD]
        return recv2[t, s]

    def wide(t, first, last):
        return jnp.concatenate([block(t, s) for s in range(first, last)], axis=1)

    with scope("A_permK"):
        loads[0].wait()
        onehot_t = onehot_of(order_ref[...])
        order_t[...] = onehot_t
        onehot = dot_nt(eye_ref[...], onehot_t).astype(BF16)
        loads[1 + K].wait()
        for half in range(2):
            rows = permuted(K, half, onehot).astype(BF16)
            for c in range(5):
                part = dot_nt(eye_ref[...], rows[:, c * 128:(c + 1) * 128])
                sendz[half, c * 128:(c + 1) * 128] = part.astype(BF16)
    with scope("A_permQ"):
        permute(Q, onehot)
    with scope("A_barrier"):
        pl.semaphore_wait(barrier, 38)
    with scope("A_sendz"):
        for half in (other, y_lo):
            column_send(sendz.at[half], recvz.at[half, head_rows(z)], s0, r0.at[half])
    with scope("A_start1Q"):
        start1(Q)
    with scope("A_permGV"):
        permute(G, onehot)
    with scope("B_start1G"):
        start1(G)
    with scope("A_permGV"):
        permute(V, onehot)
        loads[5].wait()
        index = lax.broadcasted_iota(jnp.int32, (PAD - HD, GROUP), 0)
        seg = jnp.broadcast_to(seg_ref[...].astype(F32), (PAD - HD, GROUP))
        first, second = index == 0, index == 1
        extra[0] = jnp.where(first, seg, jnp.where(second, 1.0 - seg, 0.0)).astype(BF16)
        extra[1] = jnp.where(
            first, -BIG * (1.0 - seg), jnp.where(second, -BIG * seg, 0.0)
        ).astype(BF16)

    def keys_on(half):
        with scope("wait0"):
            arrive(recvz.at[half], r0.at[half])
        to_rows(recvz.at[half], send1.at[K, half])
        plane_send(send1.at[K, half], recv1.at[K], half, s1.at[K], r1.at[K])

    with scope("B_start2Q"):
        start2(Q)
    with scope("B_keysA"):
        keys_on(other)
    with scope("B_keysB"):
        keys_on(y_lo)
    with scope("B_start1V"):
        start1(V)
    with scope("B_start2G"):
        start2(G)

    with scope("B_keysin"):
        for half in range(2):
            with scope("waitK"):
                arrive(recv1.at[K, half], r1.at[K, half])
            to_columns(recv1.at[K, half], keys_t.at[half])
        for s in range(SEQ):
            full = jnp.concatenate([block(K, s), extra[0, :, s * ROWS:(s + 1) * ROWS]], axis=0)
            rows_k[s * ROWS:(s + 1) * ROWS] = dot_nt(eye_ref[...], full).astype(BF16)
    arrived2(Q)

    def pair_of(t, qt):
        return jnp.concatenate([recv2[t, 2 * qt], recv2[t, 2 * qt + 1]], axis=1)

    def band_of(tile):
        return next(band[2:] for band in BANDS if band[0] <= tile < band[1])

    def soft_tiles(tiles):
        tops, totals, sides, scales = {}, {}, {}, {}
        steps = [
            (n, qt, slice(kt * TILE, (kt + 1) * TILE))
            for kt in range(8)
            for n, qt in enumerate(tiles)
            if band_of(qt)[0] <= kt < band_of(qt)[1]
        ]
        for qt in tiles:
            lanes = slice(qt * TILE, (qt + 1) * TILE)
            sides[qt] = jnp.concatenate([pair_of(Q, qt), extra[1, :, lanes]], axis=0)
            tops[qt] = jnp.full((8, TILE), -jnp.inf, F32)
            totals[qt] = jnp.zeros((8, TILE), F32)
        for n, qt, rows in steps:
            part = dot_nn(rows_k[rows], sides[qt])
            score[n, rows] = part
            tops[qt] = jnp.maximum(tops[qt], jnp.max(part.reshape(TILE // 8, 8, TILE), axis=0))
        for qt in tiles:
            tops[qt] = jnp.max(tops[qt], axis=0, keepdims=True) * LOG2E_ROOT
        for n, qt, rows in steps:
            part = jnp.exp2(score[n, rows] * LOG2E_ROOT - tops[qt])
            score[n, rows] = part
            totals[qt] = totals[qt] + jnp.sum(part.reshape(TILE // 8, 8, TILE), axis=0)
        for qt in tiles:
            scales[qt] = 1.0 / jnp.sum(totals[qt], axis=0, keepdims=True)
        for n, qt, rows in steps:
            probs[rows, qt * TILE:(qt + 1) * TILE] = (score[n, rows] * scales[qt]).astype(BF16)

    for pair in range(4):
        with scope("C_soft"):
            soft_tiles((pair, pair + 4))
        if pair == 0:
            with scope("B_start2V"):
                start2(V)

    def start3(t, half, pz):
        s = half * 8 + pz
        dst = recv3.at[t, half, head_rows(z)]

        @pl.when(pz != z)
        def _():
            pltpu.make_async_remote_copy(
                src_ref=send3.at[t, s],
                dst_ref=dst,
                send_sem=s3.at[t],
                recv_sem=r3.at[t, half],
                device_id=(dp, y_lo * 8 + pz),
                device_id_type=MESH,
            ).start()

        @pl.when(pz == z)
        def _():
            pltpu.make_async_copy(send3.at[t, s], dst, r3.at[t, half]).start()

    def key_side(source, band, done):
        k_first, k_last, q_first, q_last = band
        left = wide(source, 2 * q_first, 2 * q_last)
        for kt in range(k_first, k_last):
            done(
                kt,
                dot_nt(left, probs[kt * TILE:(kt + 1) * TILE, q_first * TILE:q_last * TILE]),
            )

    arrived2(G)
    with scope("C_gv"):

        def gv_done(kt, part):
            part = part.astype(BF16)
            send3[GV, 2 * kt] = part[:, :ROWS]
            send3[GV, 2 * kt + 1] = part[:, ROWS:]

        for band in BANDS:
            key_side(G, band, gv_done)
    def start3_half(t, half):
        def one(k, c):
            start3(t, half, column(k))
            return c

        lax.fori_loop(4, 12, one, 0)

    with scope("C_start3"):
        start3_half(GV, 0)
        start3_half(GV, 1)

    arrived2(V)
    tail = (lax.broadcasted_iota(jnp.int32, (PAD - HD, ROWS), 0) < 3).astype(F32).astype(BF16)
    for s in range(SEQ):
        full = jnp.concatenate([recv2[V, s], tail], axis=0)
        rows_v[s * ROWS:(s + 1) * ROWS] = dot_nt(eye_ref[...], full).astype(BF16)

    def grad_pair(pair):
        tiles = []
        for qt in (pair, pair + 4):
            k_first, k_last = band_of(qt)
            lanes = slice(qt * TILE, (qt + 1) * TILE)
            tiles.append((qt, k_first, k_last, lanes, slice(k_first * TILE, k_last * TILE)))
        sides = []
        for qt, k_first, k_last, lanes, keys in tiles:
            g_t = pair_of(G, qt)
            attended = dot_nn(wide(V, 2 * k_first, 2 * k_last), probs[keys, lanes])
            delta = -jnp.sum(g_t.astype(F32) * attended, axis=0, keepdims=True)
            high = delta.astype(BF16).astype(F32)
            middle = (delta - high).astype(BF16).astype(F32)
            low = delta - high - middle
            index = lax.broadcasted_iota(jnp.int32, (PAD - HD, TILE), 0)
            more = jnp.where(
                index == 0, high, jnp.where(index == 1, middle, jnp.where(index == 2, low, 0.0))
            ).astype(BF16)
            sides.append(jnp.concatenate([g_t, more], axis=0))
        for kt in range(8):
            for (qt, k_first, k_last, lanes, keys), g_t in zip(tiles, sides):
                if k_first <= kt < k_last:
                    rows = slice(kt * TILE, (kt + 1) * TILE)
                    part = dot_nn(rows_v[rows], g_t) * probs[rows, lanes].astype(F32)
                    probs[rows, lanes] = part.astype(BF16)

    for pair in range(4):
        with scope("D_grad"):
            grad_pair(pair)

    def start4(t, half):
        with scope("wait3"):
            arrive(recv3.at[t, half], r3.at[t, half])
        to_rows(recv3.at[t, half], send4.at[t, half])
        plane_send(send4.at[t, half], recv4.at[t], half, s4.at[t], r4.at[t])

    def gk_half(half):
        for kt in range(4 * half, 4 * half + 4):
            q_first, q_last = band_of(kt)
            part = dot_nt(
                wide(Q, 2 * q_first, 2 * q_last),
                probs[kt * TILE:(kt + 1) * TILE, q_first * TILE:q_last * TILE],
            )
            part = (part * INV_ROOT).astype(BF16)
            send3[GK, 2 * kt] = part[:, :ROWS]
            send3[GK, 2 * kt + 1] = part[:, ROWS:]
        start3_half(GK, half)

    with scope("D_gk0"):
        gk_half(0)
    for half in range(2):
        with scope("D_gq"):
            for qt in range(4 * half, 4 * half + 4):
                k_first, k_last = band_of(qt)
                grad = dot_nn(
                    wide(K, 2 * k_first, 2 * k_last),
                    probs[k_first * TILE:k_last * TILE, qt * TILE:(qt + 1) * TILE],
                )
                grad = (grad * INV_ROOT).astype(BF16)
                for j in range(2):
                    p = (2 * qt + j) % 8
                    grad_q[half, p * HD:(p + 1) * HD] = grad[:, j * ROWS:(j + 1) * ROWS]
            to_rows(grad_q.at[half], send5.at[half])
            plane_send(send5.at[half], recv5, half, s5, r5)
    with scope("D_gk1"):
        gk_half(1)
    with scope("E_start4V0"):
        start4(GV, 0)
    with scope("E_start4V1"):
        start4(GV, 1)

    def finish(t, ref):
        for half in range(2):
            with scope("wait4"):
                arrive(recv4.at[t, half], r4.at[t, half])
            rows = recv4[t, half].astype(F32).reshape(ROWS, HALF).astype(BF16)
            held[t, :, half * HALF:(half + 1) * HALF] = dot_nn(order_t[...], rows).astype(BF16)
        pltpu.make_async_copy(held.at[t], ref, load.at[t]).start()

    with scope("E_gq_on"):
        for half in (y_lo, other):
            with scope("wait5"):
                arrive(recv5.at[half], r5.at[half])
            to_columns(recv5.at[half], send6.at[half])
            column_send(send6.at[half], raw_ref.at[head_rows(half * 8 + z)], s6, r6)
    with scope("E_start4K"):
        start4(GK, 0)
        start4(GK, 1)
    with scope("E_finV"):
        finish(GV, gv_ref)
    with scope("E_finK"):
        finish(GK, gk_ref)

    with scope("E_sent"):
        def left(ref, sem):
            pltpu.make_async_copy(ref, ref, sem).wait()

        def plane_left(ref, sem):
            left(ref.at[0], sem)
            left(ref.at[1, pl.ds(0, 15)], sem)

        for t in range(4):
            plane_left(send1.at[t], s1.at[t])
        column_all = recv2.at[Q, pl.ds(0, 14)]
        left(column_all, s0)
        for t in (Q, G, V):
            left(column_all, s2.at[t])
        for t in range(2):
            left(column_all, s3.at[t])
            plane_left(send4.at[t], s4.at[t])
        plane_left(send5, s5)
        left(column_all, s6)
    with scope("E_last"):
        for t, ref in ((GV, gv_ref), (GK, gk_ref)):
            pltpu.make_async_copy(held.at[t], ref, load.at[t]).wait()
        arrive(raw_ref, r6)


def last_kernel(gv_ref, gk_ref, raw_ref, order_t, gq_out, gk_out, gv_out):
    gq_out[...] = dot_nt(order_t[...], raw_ref[...]).astype(BF16)
    gv_out[...] = gv_ref[...]
    gk_out[...] = gk_ref[...]


def on_device(queries, key_states, value_states, out_grads, row_order, segment_ids):
    out = jax.ShapeDtypeStruct((ROWS, WIDTH), BF16)
    raw = jax.ShapeDtypeStruct((WIDTH, ROWS), BF16)
    vmem = pl.BlockSpec(memory_space=pltpu.VMEM)
    anywhere = pl.BlockSpec(memory_space=pl.ANY)
    order = row_order[None, :]
    rows_form = (2, 16, 8, HALF)
    columns_form = (2, HALF, ROWS)
    dma = pltpu.SemaphoreType.DMA
    inputs = (queries, key_states, value_states, out_grads, order, segment_ids)
    parts = pl.pallas_call(
        kernel,
        out_shape=(out, out, raw, jax.ShapeDtypeStruct((ROWS, ROWS), BF16)),
        in_specs=[pl.BlockSpec(memory_space=pltpu.HBM)] * 6,
        out_specs=(anywhere, anywhere, anywhere, vmem),
        scratch_shapes=[
            pltpu.VMEM((4, ROWS, WIDTH), BF16),
            pltpu.VMEM((1, ROWS), jnp.int32),
            pltpu.VMEM((1, GROUP), jnp.int32),
            pltpu.VMEM((ROWS, ROWS), BF16),
            pltpu.VMEM(columns_form, BF16),
            pltpu.VMEM(columns_form, BF16),
            pltpu.VMEM((4, *rows_form), BF16),
            pltpu.VMEM((4, *rows_form), BF16),
            pltpu.VMEM((4, *columns_form), BF16),
            pltpu.VMEM((4, SEQ, HD, ROWS), BF16),
            pltpu.VMEM(columns_form, BF16),
            pltpu.VMEM((2, SEQ, HD, ROWS), BF16),
            pltpu.VMEM((2, *columns_form), BF16),
            pltpu.VMEM((2, *rows_form), BF16),
            pltpu.VMEM((2, *rows_form), BF16),
            pltpu.VMEM(columns_form, BF16),
            pltpu.VMEM(rows_form, BF16),
            pltpu.VMEM(rows_form, BF16),
            pltpu.VMEM(columns_form, BF16),
            pltpu.VMEM((GROUP, PAD), BF16),
            pltpu.VMEM((GROUP, PAD), BF16),
            pltpu.VMEM((2, PAD - HD, GROUP), BF16),
            pltpu.VMEM((GROUP, GROUP), BF16),
            pltpu.VMEM((2, GROUP, TILE), F32),
            dma((6,)),
            dma, dma((2,)),
            dma((4,)), dma((4, 2)),
            dma((4,)), dma((4,)),
            dma((2,)), dma((2, 2)),
            dma((2,)), dma((2, 2)),
            dma, dma((2,)),
            dma, dma,
        ],
        compiler_params=pltpu.CompilerParams(
            collective_id=0, has_side_effects=True, vmem_limit_bytes=40 << 20
        ),
    )(*(pltpu.with_memory_space_constraint(a, pltpu.HBM) for a in inputs))
    return pl.pallas_call(
        last_kernel,
        out_shape=(out, out, out),
        in_specs=[vmem] * 4,
        out_specs=(vmem, vmem, vmem),
        compiler_params=pltpu.CompilerParams(vmem_limit_bytes=8 << 20),
    )(*parts)


def solution(mesh):
    rows = P(("dp", "seq"), None)
    return jax.shard_map(
        on_device,
        mesh=mesh,
        in_specs=(rows, rows, rows, rows, P(("dp", "seq")), P("dp", None)),
        out_specs=(rows, rows, rows),
        check_vma=False,
    )
```

```python
import functools
import math

import jax
import jax.numpy as jnp
from jax import lax
from jax.experimental import pallas as pl
from jax.experimental.pallas import tpu as pltpu
from jax.sharding import PartitionSpec as P

HD = 80
ROWS = 128
WIDTH = 1280
HALF = 640
SEQ = 16
GROUP = 2048
PAD = 128
MESH = pl.DeviceIdType.MESH
BIG = 1e30
INV_ROOT = 1.0 / math.sqrt(HD)
LOG2E_ROOT = INV_ROOT * math.log2(math.e)
TILE = 256
LOW, HIGH = 6, 10
BANDS = ((0, 3, 0, 5), (3, 5, 0, 8), (5, 8, 3, 8))
K, Q, G, V = 0, 1, 2, 3
GV, GK, GQ = 0, 1, 2
FAR_FIRST = sorted(range(16), key=lambda k: -(k % 2 + (0, 1, 2, 1)[k // 2 % 4]))
BF16 = jnp.bfloat16
F32 = jnp.float32


def dot_nn(a, b):
    return lax.dot_general(a, b, (((1,), (0,)), ((), ())), preferred_element_type=F32)


def dot_nt(a, b):
    return lax.dot_general(a, b, (((1,), (1,)), ((), ())), preferred_element_type=F32)


def identity(n):
    return (
        lax.broadcasted_iota(jnp.int32, (n, n), 0) == lax.broadcasted_iota(jnp.int32, (n, n), 1)
    ).astype(F32).astype(BF16)


def scope(name):
    return jax.named_scope(name)


def onehot_of(order_row):
    return (
        lax.broadcasted_iota(jnp.int32, (ROWS, ROWS), 0)
        == jnp.broadcast_to(order_row, (ROWS, ROWS))
    ).astype(F32).astype(BF16)


def kernel(
    q_hbm, k_hbm, v_hbm, g_hbm, order_hbm, seg_hbm,
    gv_ref, gk_ref, raw_ref, order_t,
    held, order_ref, seg_ref, eye_ref,
    sendz, recvz, send1, recv1, send2, recv2, keys_t,
    send3, recv3, send4, recv4, grad_q, send5, recv5, send6,
    rows_k, rows_v, extra, probs, score,
    load, s0, r0, s1, r1, s2, r2, s3, r3, s4, r4, s5, r5, s6, r6,
):
    dp = lax.axis_index("dp")
    seq = lax.axis_index("seq")
    y_lo = lax.div(seq, 8)
    z = lax.rem(seq, 8)
    core = lax.rem(dp, 2)
    x = lax.rem(lax.div(dp, 2), 4)
    y_hi = lax.div(dp, 8)
    other = 1 - y_lo

    def near(k):
        pc = lax.rem(core + k // 8, 2)
        px = lax.rem(x + k // 2 % 4, 4)
        return lax.rem(y_hi + k % 2, 2) * 8 + px * 2 + pc

    def column(k):
        return lax.rem(z + k, 8)

    def head_rows(k):
        return pl.ds(pl.multiple_of(k * HD, 16), HD)

    def arrive(ref, sem):
        pltpu.make_async_copy(ref, ref, sem).wait()

    barrier = pltpu.get_barrier_semaphore()

    def greet(device):
        pl.semaphore_signal(barrier, inc=1, device_id=device, device_id_type=MESH)

    loads = [
        pltpu.make_async_copy(src, dst, load.at[i])
        for i, (src, dst) in enumerate(
            [(order_hbm, order_ref)]
            + [(ref, held.at[t]) for t, ref in enumerate((k_hbm, q_hbm, g_hbm, v_hbm))]
            + [(seg_hbm, seg_ref)]
        )
    ]
    for copy in loads:
        copy.start()
    with scope("A_greet"):
        for k in (4, 3, 5, 2, 6, 1, 7):
            greet((dp, y_lo * 8 + column(k)))
        for k in FAR_FIRST:
            pd = near(k)
            greet((pd, other * 8 + z))
            if k:
                greet((pd, seq))

    eye_ref[...] = identity(ROWS)

    def to_rows(src, dst):
        for c in range(5):
            part = dot_nt(eye_ref[...], src[c * 128:(c + 1) * 128])
            dst[:, :, c * 128:(c + 1) * 128] = part.reshape(16, 8, 128).astype(BF16)

    def to_columns(src, dst):
        rows = src[...].astype(F32).reshape(ROWS, HALF).astype(BF16)
        for c in range(5):
            part = dot_nt(eye_ref[...], rows[:, c * 128:(c + 1) * 128])
            dst[c * 128:(c + 1) * 128] = part.astype(BF16)

    def plane_send(src, dst, half, send_sem, recv_sem):
        for k in FAR_FIRST:
            pd = near(k)

            def remote(pd=pd):
                pltpu.make_async_remote_copy(
                    src_ref=src.at[pd],
                    dst_ref=dst.at[y_lo, dp],
                    send_sem=send_sem,
                    recv_sem=recv_sem.at[y_lo],
                    device_id=(pd, half * 8 + z),
                    device_id_type=MESH,
                ).start()

            def local():
                pltpu.make_async_copy(
                    src.at[dp], dst.at[y_lo, dp], recv_sem.at[y_lo]
                ).start()

            if k:
                remote()
            else:
                pl.when(half != y_lo)(remote)
                pl.when(half == y_lo)(local)

    def column_send(src, dst, send_sem, recv_sem):
        for k in (4, 3, 5, 2, 6, 1, 7):
            pz = column(k)
            pltpu.make_async_remote_copy(
                src_ref=src.at[head_rows(pz)],
                dst_ref=dst,
                send_sem=send_sem,
                recv_sem=recv_sem,
                device_id=(dp, y_lo * 8 + pz),
                device_id_type=MESH,
            ).start()
        pltpu.make_async_copy(src.at[head_rows(z)], dst, recv_sem).start()

    def permuted(t, half, onehot):
        return dot_nn(onehot, held[t, :, half * HALF:(half + 1) * HALF])

    def permute(t, onehot):
        loads[1 + t].wait()
        for half in range(2):
            send1[t, half] = permuted(t, half, onehot).reshape(16, 8, HALF).astype(BF16)

    def start1(t):
        for half in (other, y_lo):
            plane_send(send1.at[t, half], recv1.at[t], half, s1.at[t], r1.at[t])

    def start2(t):
        for half in (other, y_lo):
            with scope("wait1"):
                arrive(recv1.at[t, half], r1.at[t, half])
            to_columns(recv1.at[t, half], send2.at[t, half])
            column_send(send2.at[t, half], recv2.at[t, half * 8 + z], s2.at[t], r2.at[t])

    def arrived2(t):
        with scope("wait2"):
            arrive(recv2.at[t], r2.at[t])

    def block(t, s):
        if t == K:
            return keys_t[s // 8, s % 8 * HD:(s % 8 + 1) * HD]
        return recv2[t, s]

    def wide(t, first, last):
        return jnp.concatenate([block(t, s) for s in range(first, last)], axis=1)

    with scope("A_permK"):
        loads[0].wait()
        onehot_t = onehot_of(order_ref[...])
        order_t[...] = onehot_t
        onehot = dot_nt(eye_ref[...], onehot_t).astype(BF16)
        loads[1 + K].wait()
        for half in range(2):
            rows = permuted(K, half, onehot).astype(BF16)
            for c in range(5):
                part = dot_nt(eye_ref[...], rows[:, c * 128:(c + 1) * 128])
                sendz[half, c * 128:(c + 1) * 128] = part.astype(BF16)
    with scope("A_permQ"):
        permute(Q, onehot)
    with scope("A_barrier"):
        pl.semaphore_wait(barrier, 38)
    with scope("A_sendz"):
        for half in (other, y_lo):
            column_send(sendz.at[half], recvz.at[half, head_rows(z)], s0, r0.at[half])
    with scope("A_start1Q"):
        start1(Q)
    with scope("A_permGV"):
        permute(G, onehot)
    with scope("B_start1G"):
        start1(G)
    with scope("A_permGV"):
        permute(V, onehot)
        loads[5].wait()
        index = lax.broadcasted_iota(jnp.int32, (PAD - HD, GROUP), 0)
        seg = jnp.broadcast_to(seg_ref[...].astype(F32), (PAD - HD, GROUP))
        first, second = index == 0, index == 1
        extra[0] = jnp.where(first, seg, jnp.where(second, 1.0 - seg, 0.0)).astype(BF16)
        extra[1] = jnp.where(
            first, -BIG * (1.0 - seg), jnp.where(second, -BIG * seg, 0.0)
        ).astype(BF16)

    def keys_on(half):
        with scope("wait0"):
            arrive(recvz.at[half], r0.at[half])
        to_rows(recvz.at[half], send1.at[K, half])
        plane_send(send1.at[K, half], recv1.at[K], half, s1.at[K], r1.at[K])

    with scope("B_start2Q"):
        start2(Q)
    with scope("B_keysA"):
        keys_on(other)
    with scope("B_keysB"):
        keys_on(y_lo)
    with scope("B_start1V"):
        start1(V)
    with scope("B_start2G"):
        start2(G)

    with scope("B_keysin"):
        for half in range(2):
            with scope("waitK"):
                arrive(recv1.at[K, half], r1.at[K, half])
            to_columns(recv1.at[K, half], keys_t.at[half])
        for s in range(SEQ):
            full = jnp.concatenate([block(K, s), extra[0, :, s * ROWS:(s + 1) * ROWS]], axis=0)
            rows_k[s * ROWS:(s + 1) * ROWS] = dot_nt(eye_ref[...], full).astype(BF16)
    arrived2(Q)

    def pair_of(t, qt):
        return jnp.concatenate([recv2[t, 2 * qt], recv2[t, 2 * qt + 1]], axis=1)

    def band_of(tile):
        return next(band[2:] for band in BANDS if band[0] <= tile < band[1])

    def soft_tiles(tiles):
        tops, totals, sides, scales = {}, {}, {}, {}
        steps = [
            (n, qt, slice(kt * TILE, (kt + 1) * TILE))
            for kt in range(8)
            for n, qt in enumerate(tiles)
            if band_of(qt)[0] <= kt < band_of(qt)[1]
        ]
        for qt in tiles:
            lanes = slice(qt * TILE, (qt + 1) * TILE)
            sides[qt] = jnp.concatenate([pair_of(Q, qt), extra[1, :, lanes]], axis=0)
            tops[qt] = jnp.full((8, TILE), -jnp.inf, F32)
            totals[qt] = jnp.zeros((8, TILE), F32)
        for n, qt, rows in steps:
            part = dot_nn(rows_k[rows], sides[qt])
            score[n, rows] = part
            tops[qt] = jnp.maximum(tops[qt], jnp.max(part.reshape(TILE // 8, 8, TILE), axis=0))
        for qt in tiles:
            tops[qt] = jnp.max(tops[qt], axis=0, keepdims=True) * LOG2E_ROOT
        for n, qt, rows in steps:
            part = jnp.exp2(score[n, rows] * LOG2E_ROOT - tops[qt])
            score[n, rows] = part
            totals[qt] = totals[qt] + jnp.sum(part.reshape(TILE // 8, 8, TILE), axis=0)
        for qt in tiles:
            scales[qt] = 1.0 / jnp.sum(totals[qt], axis=0, keepdims=True)
        for n, qt, rows in steps:
            probs[rows, qt * TILE:(qt + 1) * TILE] = (score[n, rows] * scales[qt]).astype(BF16)

    for pair in range(4):
        with scope("C_soft"):
            soft_tiles((pair, pair + 4))
        if pair == 0:
            with scope("B_start2V"):
                start2(V)

    def key_side(source, band, done):
        k_first, k_last, q_first, q_last = band
        left = wide(source, 2 * q_first, 2 * q_last)
        for kt in range(k_first, k_last):
            done(
                kt,
                dot_nt(left, probs[kt * TILE:(kt + 1) * TILE, q_first * TILE:q_last * TILE]),
            )

    arrived2(G)
    with scope("C_gv"):

        def gv_done(kt, part):
            part = part.astype(BF16)
            send3[GV, 2 * kt] = part[:, :ROWS]
            send3[GV, 2 * kt + 1] = part[:, ROWS:]

        for band in BANDS:
            key_side(G, band, gv_done)
    def start3_half(t, half):
        src, dst = send3.at[t], recv3.at[t, half, head_rows(z)]
        for k in (4, 3, 5, 2, 6, 1, 7):
            pz = column(k)
            pltpu.make_async_remote_copy(
                src_ref=src.at[half * 8 + pz],
                dst_ref=dst,
                send_sem=s3.at[t],
                recv_sem=r3.at[t, half],
                device_id=(dp, y_lo * 8 + pz),
                device_id_type=MESH,
            ).start()
        pltpu.make_async_copy(src.at[half * 8 + z], dst, r3.at[t, half]).start()

    with scope("C_start3"):
        start3_half(GV, 0)
        start3_half(GV, 1)

    arrived2(V)
    tail = (lax.broadcasted_iota(jnp.int32, (PAD - HD, ROWS), 0) < 3).astype(F32).astype(BF16)
    for s in range(SEQ):
        full = jnp.concatenate([recv2[V, s], tail], axis=0)
        rows_v[s * ROWS:(s + 1) * ROWS] = dot_nt(eye_ref[...], full).astype(BF16)

    def grad_sides(pair):
        sides = []
        for qt in (pair, pair + 4):
            k_first, k_last = band_of(qt)
            g_t = pair_of(G, qt)
            attended = dot_nn(
                wide(V, 2 * k_first, 2 * k_last),
                probs[k_first * TILE:k_last * TILE, qt * TILE:(qt + 1) * TILE],
            )
            delta = -jnp.sum(g_t.astype(F32) * attended, axis=0, keepdims=True)
            high = delta.astype(BF16).astype(F32)
            middle = (delta - high).astype(BF16).astype(F32)
            low = delta - high - middle
            index = lax.broadcasted_iota(jnp.int32, (PAD - HD, TILE), 0)
            more = jnp.where(
                index == 0, high, jnp.where(index == 1, middle, jnp.where(index == 2, low, 0.0))
            ).astype(BF16)
            sides.append(jnp.concatenate([g_t, more], axis=0))
        return sides

    with scope("D_grad"):
        sides = grad_sides(0)
        for pair in range(4):
            ahead = grad_sides(pair + 1) if pair < 3 else None
            for kt in range(8):
                for qt, g_t in zip((pair, pair + 4), sides):
                    if band_of(qt)[0] <= kt < band_of(qt)[1]:
                        rows = slice(kt * TILE, (kt + 1) * TILE)
                        lanes = slice(qt * TILE, (qt + 1) * TILE)
                        part = dot_nn(rows_v[rows], g_t)
                        probs[rows, lanes] = (part * probs[rows, lanes].astype(F32)).astype(BF16)
            sides = ahead

    def start4(t, half):
        with scope("wait3"):
            arrive(recv3.at[t, half], r3.at[t, half])
        to_rows(recv3.at[t, half], send4.at[t, half])
        plane_send(send4.at[t, half], recv4.at[t], half, s4.at[t], r4.at[t])

    def gk_half(half):
        for kt in range(4 * half, 4 * half + 4):
            q_first, q_last = band_of(kt)
            part = dot_nt(
                wide(Q, 2 * q_first, 2 * q_last),
                probs[kt * TILE:(kt + 1) * TILE, q_first * TILE:q_last * TILE],
            )
            part = (part * INV_ROOT).astype(BF16)
            send3[GK, 2 * kt] = part[:, :ROWS]
            send3[GK, 2 * kt + 1] = part[:, ROWS:]
        start3_half(GK, half)

    with scope("D_gk0"):
        gk_half(0)
    with scope("D_gq"):
        for qt in range(8):
            k_first, k_last = band_of(qt)
            grad = dot_nn(
                wide(K, 2 * k_first, 2 * k_last),
                probs[k_first * TILE:k_last * TILE, qt * TILE:(qt + 1) * TILE],
            )
            grad = (grad * INV_ROOT).astype(BF16)
            for j in range(2):
                p = (2 * qt + j) % 8
                grad_q[qt // 4, p * HD:(p + 1) * HD] = grad[:, j * ROWS:(j + 1) * ROWS]
        for half in (y_lo, other):
            to_rows(grad_q.at[half], send5.at[half])
            plane_send(send5.at[half], recv5, half, s5, r5)
    with scope("D_gk1"):
        gk_half(1)
    with scope("E_start4V0"):
        start4(GV, 0)
    with scope("E_start4V1"):
        start4(GV, 1)

    def finish(t, ref):
        for half in range(2):
            with scope("wait4"):
                arrive(recv4.at[t, half], r4.at[t, half])
            rows = recv4[t, half].astype(F32).reshape(ROWS, HALF).astype(BF16)
            held[t, :, half * HALF:(half + 1) * HALF] = dot_nn(order_t[...], rows).astype(BF16)
        pltpu.make_async_copy(held.at[t], ref, load.at[t]).start()

    with scope("E_gq_on"):
        for half in (y_lo, other):
            with scope("wait5"):
                arrive(recv5.at[half], r5.at[half])
            to_columns(recv5.at[half], send6.at[half])
            column_send(send6.at[half], raw_ref.at[head_rows(half * 8 + z)], s6, r6)
    with scope("E_start4K"):
        start4(GK, 0)
        start4(GK, 1)
    with scope("E_finV"):
        finish(GV, gv_ref)
    with scope("E_finK"):
        finish(GK, gk_ref)

    with scope("E_sent"):
        def left(ref, sem):
            pltpu.make_async_copy(ref, ref, sem).wait()

        def plane_left(ref, sem):
            left(ref.at[0], sem)
            left(ref.at[1, pl.ds(0, 15)], sem)

        for t in range(4):
            plane_left(send1.at[t], s1.at[t])
        column_all = recv2.at[Q, pl.ds(0, 14)]
        left(column_all, s0)
        for t in (Q, G, V):
            left(column_all, s2.at[t])
        for t in range(2):
            left(column_all, s3.at[t])
            plane_left(send4.at[t], s4.at[t])
        plane_left(send5, s5)
        left(column_all, s6)
    with scope("E_last"):
        for t, ref in ((GV, gv_ref), (GK, gk_ref)):
            pltpu.make_async_copy(held.at[t], ref, load.at[t]).wait()
        arrive(raw_ref, r6)


def last_kernel(gv_ref, gk_ref, raw_ref, order_t, gq_out, gk_out, gv_out):
    gq_out[...] = dot_nt(order_t[...], raw_ref[...]).astype(BF16)
    gv_out[...] = gv_ref[...]
    gk_out[...] = gk_ref[...]


def on_device(queries, key_states, value_states, out_grads, row_order, segment_ids):
    out = jax.ShapeDtypeStruct((ROWS, WIDTH), BF16)
    raw = jax.ShapeDtypeStruct((WIDTH, ROWS), BF16)
    vmem = pl.BlockSpec(memory_space=pltpu.VMEM)
    anywhere = pl.BlockSpec(memory_space=pl.ANY)
    order = row_order[None, :]
    rows_form = (2, 16, 8, HALF)
    columns_form = (2, HALF, ROWS)
    dma = pltpu.SemaphoreType.DMA
    inputs = (queries, key_states, value_states, out_grads, order, segment_ids)
    parts = pl.pallas_call(
        kernel,
        out_shape=(out, out, raw, jax.ShapeDtypeStruct((ROWS, ROWS), BF16)),
        in_specs=[pl.BlockSpec(memory_space=pltpu.HBM)] * 6,
        out_specs=(anywhere, anywhere, anywhere, vmem),
        scratch_shapes=[
            pltpu.VMEM((4, ROWS, WIDTH), BF16),
            pltpu.VMEM((1, ROWS), jnp.int32),
            pltpu.VMEM((1, GROUP), jnp.int32),
            pltpu.VMEM((ROWS, ROWS), BF16),
            pltpu.VMEM(columns_form, BF16),
            pltpu.VMEM(columns_form, BF16),
            pltpu.VMEM((4, *rows_form), BF16),
            pltpu.VMEM((4, *rows_form), BF16),
            pltpu.VMEM((4, *columns_form), BF16),
            pltpu.VMEM((4, SEQ, HD, ROWS), BF16),
            pltpu.VMEM(columns_form, BF16),
            pltpu.VMEM((2, SEQ, HD, ROWS), BF16),
            pltpu.VMEM((2, *columns_form), BF16),
            pltpu.VMEM((2, *rows_form), BF16),
            pltpu.VMEM((2, *rows_form), BF16),
            pltpu.VMEM(columns_form, BF16),
            pltpu.VMEM(rows_form, BF16),
            pltpu.VMEM(rows_form, BF16),
            pltpu.VMEM(columns_form, BF16),
            pltpu.VMEM((GROUP, PAD), BF16),
            pltpu.VMEM((GROUP, PAD), BF16),
            pltpu.VMEM((2, PAD - HD, GROUP), BF16),
            pltpu.VMEM((GROUP, GROUP), BF16),
            pltpu.VMEM((2, GROUP, TILE), F32),
            dma((6,)),
            dma, dma((2,)),
            dma((4,)), dma((4, 2)),
            dma((4,)), dma((4,)),
            dma((2,)), dma((2, 2)),
            dma((2,)), dma((2, 2)),
            dma, dma((2,)),
            dma, dma,
        ],
        compiler_params=pltpu.CompilerParams(
            collective_id=0, has_side_effects=True, vmem_limit_bytes=40 << 20,
        ),
    )(*(pltpu.with_memory_space_constraint(a, pltpu.HBM) for a in inputs))
    return pl.pallas_call(
        last_kernel,
        out_shape=(out, out, out),
        in_specs=[vmem] * 4,
        out_specs=(vmem, vmem, vmem),
        compiler_params=pltpu.CompilerParams(vmem_limit_bytes=8 << 20),
    )(*parts)


def solution(mesh):
    rows = P(("dp", "seq"), None)
    return jax.shard_map(
        on_device,
        mesh=mesh,
        in_specs=(rows, rows, rows, rows, P(("dp", "seq")), P("dp", None)),
        out_specs=(rows, rows, rows),
        check_vma=False,
    )
```

```python
import functools
import math

import jax
import jax.numpy as jnp
from jax import lax
from jax.experimental import pallas as pl
from jax.experimental.pallas import tpu as pltpu
from jax.sharding import PartitionSpec as P

HD = 80
ROWS = 128
WIDTH = 1280
HALF = 640
SEQ = 16
GROUP = 2048
PAD = 128
MESH = pl.DeviceIdType.MESH
BIG = 1e30
INV_ROOT = 1.0 / math.sqrt(HD)
LOG2E_ROOT = INV_ROOT * math.log2(math.e)
TILE = 256
LOW, HIGH = 6, 10
BANDS = ((0, 3, 0, 5), (3, 5, 0, 8), (5, 8, 3, 8))
K, Q, G, V = 0, 1, 2, 3
GV, GK, GQ = 0, 1, 2
FAR_FIRST = sorted(range(16), key=lambda k: -(k % 2 + (0, 1, 2, 1)[k // 2 % 4]))
BF16 = jnp.bfloat16
F32 = jnp.float32


def dot_nn(a, b):
    return lax.dot_general(a, b, (((1,), (0,)), ((), ())), preferred_element_type=F32)


def dot_nt(a, b):
    return lax.dot_general(a, b, (((1,), (1,)), ((), ())), preferred_element_type=F32)


def identity(n):
    return (
        lax.broadcasted_iota(jnp.int32, (n, n), 0) == lax.broadcasted_iota(jnp.int32, (n, n), 1)
    ).astype(F32).astype(BF16)


def scope(name):
    return jax.named_scope(name)


def onehot_of(order_row):
    return (
        lax.broadcasted_iota(jnp.int32, (ROWS, ROWS), 0)
        == jnp.broadcast_to(order_row, (ROWS, ROWS))
    ).astype(F32).astype(BF16)


def kernel(
    q_hbm, k_hbm, v_hbm, g_hbm, order_hbm, seg_hbm,
    gv_ref, gk_ref, raw_ref, order_t,
    held, order_ref, seg_ref, eye_ref,
    sendz, recvz, send1, recv1, send2, recv2, keys_t,
    send3, recv3, send4, recv4, grad_q, send5, recv5, send6,
    rows_k, rows_v, extra, probs, score,
    load, s0, r0, s1, r1, s2, r2, s3, r3, s4, r4, s5, r5, s6, r6,
):
    dp = lax.axis_index("dp")
    seq = lax.axis_index("seq")
    y_lo = lax.div(seq, 8)
    z = lax.rem(seq, 8)
    core = lax.rem(dp, 2)
    x = lax.rem(lax.div(dp, 2), 4)
    y_hi = lax.div(dp, 8)
    other = 1 - y_lo

    def near(k):
        pc = lax.rem(core + k // 8, 2)
        px = lax.rem(x + k // 2 % 4, 4)
        return lax.rem(y_hi + k % 2, 2) * 8 + px * 2 + pc

    def column(k):
        return lax.rem(z + k, 8)

    def head_rows(k):
        return pl.ds(pl.multiple_of(k * HD, 16), HD)

    def arrive(ref, sem):
        pltpu.make_async_copy(ref, ref, sem).wait()

    barrier = pltpu.get_barrier_semaphore()

    def greet(device):
        pl.semaphore_signal(barrier, inc=1, device_id=device, device_id_type=MESH)

    loads = [
        pltpu.make_async_copy(src, dst, load.at[i])
        for i, (src, dst) in enumerate(
            [(order_hbm, order_ref)]
            + [(ref, held.at[t]) for t, ref in enumerate((k_hbm, q_hbm, g_hbm, v_hbm))]
            + [(seg_hbm, seg_ref)]
        )
    ]
    for copy in loads:
        copy.start()
    with scope("A_greet"):
        for k in (4, 3, 5, 2, 6, 1, 7):
            greet((dp, y_lo * 8 + column(k)))
        for k in FAR_FIRST:
            pd = near(k)
            greet((pd, other * 8 + z))
            if k:
                greet((pd, seq))

    eye_ref[...] = identity(ROWS)

    def to_rows(src, dst):
        for c in range(5):
            part = dot_nt(eye_ref[...], src[c * 128:(c + 1) * 128])
            dst[:, :, c * 128:(c + 1) * 128] = part.reshape(16, 8, 128).astype(BF16)

    def to_columns(src, dst):
        rows = src[...].astype(F32).reshape(ROWS, HALF).astype(BF16)
        for c in range(5):
            part = dot_nt(eye_ref[...], rows[:, c * 128:(c + 1) * 128])
            dst[c * 128:(c + 1) * 128] = part.astype(BF16)

    def plane_send(src, dst, half, send_sem, recv_sem):
        for k in FAR_FIRST:
            pd = near(k)

            def remote(pd=pd):
                pltpu.make_async_remote_copy(
                    src_ref=src.at[pd],
                    dst_ref=dst.at[y_lo, dp],
                    send_sem=send_sem,
                    recv_sem=recv_sem.at[y_lo],
                    device_id=(pd, half * 8 + z),
                    device_id_type=MESH,
                ).start()

            def local():
                pltpu.make_async_copy(
                    src.at[dp], dst.at[y_lo, dp], recv_sem.at[y_lo]
                ).start()

            if k:
                remote()
            else:
                pl.when(half != y_lo)(remote)
                pl.when(half == y_lo)(local)

    def column_send(src, dst, send_sem, recv_sem):
        for k in (4, 3, 5, 2, 6, 1, 7):
            pz = column(k)
            pltpu.make_async_remote_copy(
                src_ref=src.at[head_rows(pz)],
                dst_ref=dst,
                send_sem=send_sem,
                recv_sem=recv_sem,
                device_id=(dp, y_lo * 8 + pz),
                device_id_type=MESH,
            ).start()
        pltpu.make_async_copy(src.at[head_rows(z)], dst, recv_sem).start()

    def permuted(t, half, onehot):
        return dot_nn(onehot, held[t, :, half * HALF:(half + 1) * HALF])

    def permute(t, onehot):
        loads[1 + t].wait()
        for half in range(2):
            send1[t, half] = permuted(t, half, onehot).reshape(16, 8, HALF).astype(BF16)

    def start1(t):
        for half in (other, y_lo):
            plane_send(send1.at[t, half], recv1.at[t], half, s1.at[t], r1.at[t])

    def start2(t):
        for half in (other, y_lo):
            with scope("wait1"):
                arrive(recv1.at[t, half], r1.at[t, half])
            to_columns(recv1.at[t, half], send2.at[t, half])
            column_send(send2.at[t, half], recv2.at[t, half * 8 + z], s2.at[t], r2.at[t])

    def arrived2(t):
        with scope("wait2"):
            arrive(recv2.at[t], r2.at[t])

    def block(t, s):
        if t == K:
            return keys_t[s // 8, s % 8 * HD:(s % 8 + 1) * HD]
        return recv2[t, s]

    def wide(t, first, last):
        return jnp.concatenate([block(t, s) for s in range(first, last)], axis=1)

    with scope("A_permK"):
        loads[0].wait()
        onehot_t = onehot_of(order_ref[...])
        order_t[...] = onehot_t
        onehot = dot_nt(eye_ref[...], onehot_t).astype(BF16)
        loads[1 + K].wait()
        for half in range(2):
            rows = permuted(K, half, onehot).astype(BF16)
            for c in range(5):
                part = dot_nt(eye_ref[...], rows[:, c * 128:(c + 1) * 128])
                sendz[half, c * 128:(c + 1) * 128] = part.astype(BF16)
    with scope("A_permQ"):
        permute(Q, onehot)
    with scope("A_barrier"):
        pl.semaphore_wait(barrier, 38)
    with scope("A_sendz"):
        for half in (other, y_lo):
            column_send(sendz.at[half], recvz.at[half, head_rows(z)], s0, r0.at[half])
    with scope("A_start1Q"):
        start1(Q)
    with scope("A_permGV"):
        permute(G, onehot)
    with scope("B_start1G"):
        start1(G)
    with scope("A_permGV"):
        permute(V, onehot)
        loads[5].wait()
        index = lax.broadcasted_iota(jnp.int32, (PAD - HD, GROUP), 0)
        seg = jnp.broadcast_to(seg_ref[...].astype(F32), (PAD - HD, GROUP))
        first, second = index == 0, index == 1
        extra[0] = jnp.where(first, seg, jnp.where(second, 1.0 - seg, 0.0)).astype(BF16)
        extra[1] = jnp.where(
            first, -BIG * (1.0 - seg), jnp.where(second, -BIG * seg, 0.0)
        ).astype(BF16)

    def keys_on(half):
        with scope("wait0"):
            arrive(recvz.at[half], r0.at[half])
        to_rows(recvz.at[half], send1.at[K, half])
        plane_send(send1.at[K, half], recv1.at[K], half, s1.at[K], r1.at[K])

    with scope("B_start2Q"):
        start2(Q)
    with scope("B_keysA"):
        keys_on(other)
    with scope("B_keysB"):
        keys_on(y_lo)
    with scope("B_start1V"):
        start1(V)
    with scope("B_start2G"):
        start2(G)

    with scope("B_keysin"):
        for half in range(2):
            with scope("waitK"):
                arrive(recv1.at[K, half], r1.at[K, half])
            to_columns(recv1.at[K, half], keys_t.at[half])
        for s in range(SEQ):
            full = jnp.concatenate([block(K, s), extra[0, :, s * ROWS:(s + 1) * ROWS]], axis=0)
            rows_k[s * ROWS:(s + 1) * ROWS] = dot_nt(eye_ref[...], full).astype(BF16)
    arrived2(Q)

    def pair_of(t, qt):
        return jnp.concatenate([recv2[t, 2 * qt], recv2[t, 2 * qt + 1]], axis=1)

    def band_of(tile):
        return next(band[2:] for band in BANDS if band[0] <= tile < band[1])

    def soft_tiles(tiles):
        tops, totals, sides, scales = {}, {}, {}, {}
        steps = [
            (n, qt, slice(kt * TILE, (kt + 1) * TILE))
            for kt in range(8)
            for n, qt in enumerate(tiles)
            if band_of(qt)[0] <= kt < band_of(qt)[1]
        ]
        for qt in tiles:
            lanes = slice(qt * TILE, (qt + 1) * TILE)
            sides[qt] = jnp.concatenate([pair_of(Q, qt), extra[1, :, lanes]], axis=0)
            tops[qt] = jnp.full((8, TILE), -jnp.inf, F32)
            totals[qt] = jnp.zeros((8, TILE), F32)
        for n, qt, rows in steps:
            part = dot_nn(rows_k[rows], sides[qt])
            score[n, rows] = part
            tops[qt] = jnp.maximum(tops[qt], jnp.max(part.reshape(TILE // 8, 8, TILE), axis=0))
        for qt in tiles:
            tops[qt] = jnp.max(tops[qt], axis=0, keepdims=True) * LOG2E_ROOT
        for n, qt, rows in steps:
            part = jnp.exp2(score[n, rows] * LOG2E_ROOT - tops[qt])
            score[n, rows] = part
            totals[qt] = totals[qt] + jnp.sum(part.reshape(TILE // 8, 8, TILE), axis=0)
        for qt in tiles:
            scales[qt] = 1.0 / jnp.sum(totals[qt], axis=0, keepdims=True)
        for n, qt, rows in steps:
            probs[rows, qt * TILE:(qt + 1) * TILE] = (score[n, rows] * scales[qt]).astype(BF16)

    for pair in range(4):
        with scope("C_soft"):
            soft_tiles((pair, pair + 4))
        if pair == 0:
            with scope("B_start2V"):
                start2(V)

    def key_side(source, band, done):
        k_first, k_last, q_first, q_last = band
        left = wide(source, 2 * q_first, 2 * q_last)
        for kt in range(k_first, k_last):
            done(
                kt,
                dot_nt(left, probs[kt * TILE:(kt + 1) * TILE, q_first * TILE:q_last * TILE]),
            )

    arrived2(G)
    with scope("C_gv"):

        def gv_done(kt, part):
            part = part.astype(BF16)
            send3[GV, 2 * kt] = part[:, :ROWS]
            send3[GV, 2 * kt + 1] = part[:, ROWS:]

        for band in BANDS:
            key_side(G, band, gv_done)
    def start3_half(t, half):
        src, dst = send3.at[t], recv3.at[t, half, head_rows(z)]
        for k in (4, 3, 5, 2, 6, 1, 7):
            pz = column(k)
            pltpu.make_async_remote_copy(
                src_ref=src.at[half * 8 + pz],
                dst_ref=dst,
                send_sem=s3.at[t],
                recv_sem=r3.at[t, half],
                device_id=(dp, y_lo * 8 + pz),
                device_id_type=MESH,
            ).start()
        pltpu.make_async_copy(src.at[half * 8 + z], dst, r3.at[t, half]).start()

    with scope("C_start3"):
        start3_half(GV, 0)
        start3_half(GV, 1)

    arrived2(V)
    tail = (lax.broadcasted_iota(jnp.int32, (PAD - HD, ROWS), 0) < 3).astype(F32).astype(BF16)
    for s in range(SEQ):
        full = jnp.concatenate([recv2[V, s], tail], axis=0)
        rows_v[s * ROWS:(s + 1) * ROWS] = dot_nt(eye_ref[...], full).astype(BF16)

    def grad_sides(pair):
        sides = []
        for qt in (pair, pair + 4):
            k_first, k_last = band_of(qt)
            g_t = pair_of(G, qt)
            attended = dot_nn(
                wide(V, 2 * k_first, 2 * k_last),
                probs[k_first * TILE:k_last * TILE, qt * TILE:(qt + 1) * TILE],
            )
            delta = -jnp.sum(g_t.astype(F32) * attended, axis=0, keepdims=True)
            high = delta.astype(BF16).astype(F32)
            middle = (delta - high).astype(BF16).astype(F32)
            low = delta - high - middle
            index = lax.broadcasted_iota(jnp.int32, (PAD - HD, TILE), 0)
            more = jnp.where(
                index == 0, high, jnp.where(index == 1, middle, jnp.where(index == 2, low, 0.0))
            ).astype(BF16)
            sides.append(jnp.concatenate([g_t, more], axis=0))
        return sides

    with scope("D_grad"):
        sides = grad_sides(0)
        for pair in range(4):
            ahead = grad_sides(pair + 1) if pair < 3 else None
            for kt in range(8):
                for qt, g_t in zip((pair, pair + 4), sides):
                    if band_of(qt)[0] <= kt < band_of(qt)[1]:
                        rows = slice(kt * TILE, (kt + 1) * TILE)
                        lanes = slice(qt * TILE, (qt + 1) * TILE)
                        part = dot_nn(rows_v[rows], g_t)
                        probs[rows, lanes] = (part * probs[rows, lanes].astype(F32)).astype(BF16)
            sides = ahead

    def start4(t, half):
        with scope("wait3"):
            arrive(recv3.at[t, half], r3.at[t, half])
        to_rows(recv3.at[t, half], send4.at[t, half])
        plane_send(send4.at[t, half], recv4.at[t], half, s4.at[t], r4.at[t])

    def gk_half(half):
        for kt in range(4 * half, 4 * half + 4):
            q_first, q_last = band_of(kt)
            part = dot_nt(
                wide(Q, 2 * q_first, 2 * q_last),
                probs[kt * TILE:(kt + 1) * TILE, q_first * TILE:q_last * TILE],
            )
            part = (part * INV_ROOT).astype(BF16)
            send3[GK, 2 * kt] = part[:, :ROWS]
            send3[GK, 2 * kt + 1] = part[:, ROWS:]
        start3_half(GK, half)

    with scope("D_gk0"):
        gk_half(0)
    with scope("D_gq"):
        for qt in range(8):
            k_first, k_last = band_of(qt)
            grad = dot_nn(
                wide(K, 2 * k_first, 2 * k_last),
                probs[k_first * TILE:k_last * TILE, qt * TILE:(qt + 1) * TILE],
            )
            grad = (grad * INV_ROOT).astype(BF16)
            for j in range(2):
                p = (2 * qt + j) % 8
                grad_q[qt // 4, p * HD:(p + 1) * HD] = grad[:, j * ROWS:(j + 1) * ROWS]
        for half in (y_lo, other):
            to_rows(grad_q.at[half], send5.at[half])
            plane_send(send5.at[half], recv5, half, s5, r5)
    with scope("D_gk1"):
        gk_half(1)
    with scope("E_start4V0"):
        start4(GV, 0)
    with scope("E_start4V1"):
        start4(GV, 1)

    def finish(t, ref):
        for half in range(2):
            with scope("wait4"):
                arrive(recv4.at[t, half], r4.at[t, half])
            rows = recv4[t, half].astype(F32).reshape(ROWS, HALF).astype(BF16)
            held[t, :, half * HALF:(half + 1) * HALF] = dot_nn(order_t[...], rows).astype(BF16)
        pltpu.make_async_copy(held.at[t], ref, load.at[t]).start()

    with scope("E_gq_on"):
        for half in (y_lo, other):
            with scope("wait5"):
                arrive(recv5.at[half], r5.at[half])
            to_columns(recv5.at[half], send6.at[half])
            column_send(send6.at[half], raw_ref.at[head_rows(half * 8 + z)], s6, r6)
    with scope("E_start4K"):
        start4(GK, 0)
        start4(GK, 1)
    with scope("E_finV"):
        finish(GV, gv_ref)
    with scope("E_finK"):
        finish(GK, gk_ref)

    with scope("E_sent"):
        def left(ref, sem):
            pltpu.make_async_copy(ref, ref, sem).wait()

        def plane_left(ref, sem):
            left(ref.at[0], sem)
            left(ref.at[1, pl.ds(0, 15)], sem)

        for t in range(4):
            plane_left(send1.at[t], s1.at[t])
        column_all = recv2.at[Q, pl.ds(0, 14)]
        left(column_all, s0)
        for t in (Q, G, V):
            left(column_all, s2.at[t])
        for t in range(2):
            left(column_all, s3.at[t])
            plane_left(send4.at[t], s4.at[t])
        plane_left(send5, s5)
        left(column_all, s6)
    with scope("E_last"):
        for t, ref in ((GV, gv_ref), (GK, gk_ref)):
            pltpu.make_async_copy(held.at[t], ref, load.at[t]).wait()
        arrive(raw_ref, r6)


def last_kernel(gv_ref, gk_ref, raw_ref, order_t, gq_out, gk_out, gv_out, done, go):
    copies = [
        pltpu.make_async_copy(gv_ref, gv_out, go.at[0]),
        pltpu.make_async_copy(gk_ref, gk_out, go.at[1]),
        pltpu.make_async_copy(done, gq_out, go.at[2]),
    ]
    copies[0].start()
    copies[1].start()
    done[...] = dot_nt(order_t[...], raw_ref[...]).astype(BF16)
    copies[2].start()
    for copy in copies:
        copy.wait()


def on_device(queries, key_states, value_states, out_grads, row_order, segment_ids):
    out = jax.ShapeDtypeStruct((ROWS, WIDTH), BF16)
    raw = jax.ShapeDtypeStruct((WIDTH, ROWS), BF16)
    vmem = pl.BlockSpec(memory_space=pltpu.VMEM)
    anywhere = pl.BlockSpec(memory_space=pl.ANY)
    order = row_order[None, :]
    rows_form = (2, 16, 8, HALF)
    columns_form = (2, HALF, ROWS)
    dma = pltpu.SemaphoreType.DMA
    inputs = (queries, key_states, value_states, out_grads, order, segment_ids)
    parts = pl.pallas_call(
        kernel,
        out_shape=(out, out, raw, jax.ShapeDtypeStruct((ROWS, ROWS), BF16)),
        in_specs=[pl.BlockSpec(memory_space=pltpu.HBM)] * 6,
        out_specs=(anywhere, anywhere, anywhere, vmem),
        scratch_shapes=[
            pltpu.VMEM((4, ROWS, WIDTH), BF16),
            pltpu.VMEM((1, ROWS), jnp.int32),
            pltpu.VMEM((1, GROUP), jnp.int32),
            pltpu.VMEM((ROWS, ROWS), BF16),
            pltpu.VMEM(columns_form, BF16),
            pltpu.VMEM(columns_form, BF16),
            pltpu.VMEM((4, *rows_form), BF16),
            pltpu.VMEM((4, *rows_form), BF16),
            pltpu.VMEM((4, *columns_form), BF16),
            pltpu.VMEM((4, SEQ, HD, ROWS), BF16),
            pltpu.VMEM(columns_form, BF16),
            pltpu.VMEM((2, SEQ, HD, ROWS), BF16),
            pltpu.VMEM((2, *columns_form), BF16),
            pltpu.VMEM((2, *rows_form), BF16),
            pltpu.VMEM((2, *rows_form), BF16),
            pltpu.VMEM(columns_form, BF16),
            pltpu.VMEM(rows_form, BF16),
            pltpu.VMEM(rows_form, BF16),
            pltpu.VMEM(columns_form, BF16),
            pltpu.VMEM((GROUP, PAD), BF16),
            pltpu.VMEM((GROUP, PAD), BF16),
            pltpu.VMEM((2, PAD - HD, GROUP), BF16),
            pltpu.VMEM((GROUP, GROUP), BF16),
            pltpu.VMEM((2, GROUP, TILE), F32),
            dma((6,)),
            dma, dma((2,)),
            dma((4,)), dma((4, 2)),
            dma((4,)), dma((4,)),
            dma((2,)), dma((2, 2)),
            dma((2,)), dma((2, 2)),
            dma, dma((2,)),
            dma, dma,
        ],
        compiler_params=pltpu.CompilerParams(
            collective_id=0, has_side_effects=True, vmem_limit_bytes=40 << 20,
        ),
    )(*(pltpu.with_memory_space_constraint(a, pltpu.HBM) for a in inputs))
    return pl.pallas_call(
        last_kernel,
        out_shape=(out, out, out),
        in_specs=[anywhere, anywhere, vmem, vmem],
        out_specs=(anywhere, anywhere, anywhere),
        scratch_shapes=[pltpu.VMEM((ROWS, WIDTH), BF16), dma((3,))],
        compiler_params=pltpu.CompilerParams(vmem_limit_bytes=8 << 20),
    )(*parts)


def solution(mesh):
    rows = P(("dp", "seq"), None)
    return jax.shard_map(
        on_device,
        mesh=mesh,
        in_specs=(rows, rows, rows, rows, P(("dp", "seq")), P("dp", None)),
        out_specs=(rows, rows, rows),
        check_vma=False,
    )
```
